256 devices in a mesh: space: 64 (over x, z, core), slab: 4 (over y).
Axes of the slice: x: 4, y: 4, z: 8, core: 2. Of those that a mesh axis runs over, the one named last changes fastest.
Arguments:
- tokens: float32 [65536, 512], P(('space', 'slab')), may hold values from -6 to 6
- gain: float32 [512], replicated, may hold values from 0.25 to 1.75
- query_weight: float32 [512, 512], replicated, may hold values from -3.1 to 3.1
- key_weight: float32 [512, 512], replicated, may hold values from -0.25 to 0.25
- value_weight: float32 [512, 512], replicated, may hold values from -0.25 to 0.25
- output_weight: float32 [512, 512], replicated, may hold values from -0.25 to 0.25
- neighbour_list: int32 [512, 3], P(('space', 'slab')), may hold values from 0 to 5, as said below
- neighbour_count: int32 [512], P(('space', 'slab')), may hold values from 1 to 3, as said below
- cotangent: float32 [65536, 512], P(('space', 'slab')), may hold values from -6 to 6
Outputs:
- result: float32 [65536, 512], P(('space', 'slab'))
- d_tokens: float32 [65536, 512], P(('space', 'slab'))
- d_gain: float32 [512], replicated
- d_query: float32 [512, 512], replicated
- d_key: float32 [512, 512], replicated
- d_value: float32 [512, 512], replicated
- d_output: float32 [512, 512], replicated
The draws below stay inside these ranges and needn't reach their ends.
Inputs may be any that keep to these rules, and one draw needn't show every extreme that they name: `neighbour_list`: each row holds distinct window indices, never the patch's own index 2 + p % 2. Only the first neighbour_count[p] entries of a row are live.
All inputs are finite; a program needn't handle non-finite values.
Results may differ from the reference program's by a relative error of at most 0.0003.
Values sent between devices are 32-bit elements; how exact they have to be, the bound alone decides.
A program may use at most 128 MiB of HBM per device.

```python
import jax
import jax.numpy as jnp
from jax import lax

D = 512
HEADS = 8
PT = 128
NB = 3
P_DEV = 2
PATCHES = 512
TOKENS = 65536
N_SPACE = 64
N_SLAB = 4


def draw_query_weight(key, part):
    return jnp.clip(jax.random.normal(key, (D, D), jnp.float32), -6.0, 6.0) * D ** (-0.5)


def draw_neighbour_list(key, part):
    candidates = 3 * P_DEV - 1
    row_keys = jax.random.split(jax.random.fold_in(key, 11), PATCHES)
    picked = jax.vmap(lambda row_key: jax.random.permutation(row_key, candidates))(row_keys)[:, :NB]
    own_blocks = P_DEV + jnp.arange(PATCHES, dtype=jnp.int32) % P_DEV
    return jnp.where(picked >= own_blocks[:, None], picked + 1, picked).astype(jnp.int32)


def draw_neighbour_count(key, part):
    base = jax.random.randint(jax.random.fold_in(key, 5), (PATCHES,), 1, NB + 1)
    start = jax.random.randint(jax.random.fold_in(key, 3), (), 0, PATCHES)
    distance = (jnp.arange(PATCHES, dtype=jnp.int32) - start) % PATCHES
    return jnp.where(distance < PATCHES // 8, NB, base).astype(jnp.int32)


def steps_of(own_key, shape, cuts, smallest, high):
    loudness, own = 1.0, jax.random.fold_in(own_key, 6)
    for position, shards_of in cuts:
        steps = jnp.exp(jax.random.uniform(jax.random.fold_in(own, position), (shards_of,), jnp.float32, smallest / len(cuts), high / len(cuts)))
        loudness = loudness * jnp.repeat(steps, shape[position] // shards_of).reshape([-1 if axis == position else 1 for axis in range(len(shape))])
    return loudness


def noise(own_key, extent, spread, reach, cuts=(), kind=jnp.bfloat16):
    drawn = spread * jax.random.normal(own_key, extent, jnp.float32)
    if cuts:
        drawn = drawn * steps_of(own_key, extent, cuts, -0.22, 0.18)
    return jnp.clip(drawn, -reach, reach).astype(kind)


def setup_inputs(seed: int = 0) -> dict:
    streams_of = jax.random.split(jax.random.key(seed), 10)
    tokens = noise(streams_of[0], (TOKENS, D), 1.0, 6.0, ((0, 256),), jnp.float32)
    gain = jnp.clip(1.0 + 0.15 * jax.random.normal(streams_of[1], (D,), jnp.float32), 0.25, 1.75)
    query_weight = draw_query_weight(jax.random.fold_in(streams_of[9], 71), 0)
    key_weight = noise(streams_of[3], (D, D), D ** -0.5, 0.25, (), jnp.float32)
    value_weight = noise(streams_of[4], (D, D), D ** -0.5, 0.25, (), jnp.float32)
    output_weight = noise(streams_of[5], (D, D), D ** -0.5, 0.25, (), jnp.float32)
    neighbour_list = draw_neighbour_list(jax.random.fold_in(streams_of[9], 71), 0)
    neighbour_count = draw_neighbour_count(jax.random.fold_in(streams_of[9], 71), 0)
    cotangent = noise(streams_of[8], (TOKENS, D), 1.0, 6.0, ((0, 256),), jnp.float32)
    return {"tokens": tokens, "gain": gain, "query_weight": query_weight, "key_weight": key_weight, "value_weight": value_weight, "output_weight": output_weight, "neighbour_list": neighbour_list, "neighbour_count": neighbour_count, "cotangent": cotangent}


def matmul(left, right):
    return jnp.dot(left, right, precision=lax.Precision.HIGHEST, preferred_element_type=jnp.float32)

def normalize(tokens, gain):
    row_mean = lax.optimization_barrier(jnp.mean(tokens, axis=1, keepdims=True))
    centred = tokens - row_mean
    variance = lax.optimization_barrier(jnp.mean(centred * centred, axis=1, keepdims=True))
    return centred * lax.rsqrt(variance + 1e-05) * gain[None, :]

def attention(query, key_win, value_win, block_index, live_mask):
    patch_count = block_index.shape[0]
    model_width = query.shape[1]
    head_dim = model_width // HEADS
    picked_keys = key_win.reshape(-1, PT, model_width)[block_index].reshape(patch_count, -1, HEADS, head_dim)
    picked_values = value_win.reshape(-1, PT, model_width)[block_index].reshape(patch_count, -1, HEADS, head_dim)
    query_blocks = query.reshape(patch_count, PT, HEADS, head_dim)
    scores = jnp.einsum('pqhd,pkhd->phqk', query_blocks, picked_keys, precision=lax.Precision.HIGHEST) * head_dim ** (-0.5)
    key_mask = jnp.repeat(live_mask, PT, axis=1)
    scores = jnp.where(key_mask[:, None, None, :], scores, -1e+30)
    row_max = lax.optimization_barrier(jnp.max(scores, axis=3, keepdims=True))
    weights = jnp.exp(scores - row_max)
    probability = weights / lax.optimization_barrier(jnp.sum(weights, axis=3, keepdims=True))
    mixed = jnp.einsum('phqk,pkhd->pqhd', probability, picked_values, precision=lax.Precision.HIGHEST)
    return mixed.reshape(patch_count * PT, model_width)

def reference(tokens, gain, query_weight, key_weight, value_weight, output_weight, neighbour_list, neighbour_count, cotangent):
    device_count = N_SPACE * N_SLAB
    own_blocks = P_DEV + jnp.arange(PATCHES, dtype=jnp.int32) % P_DEV
    block_index = jnp.concatenate([own_blocks[:, None], neighbour_list], axis=1).reshape(device_count, P_DEV, NB + 1)
    slot_ids = jnp.arange(NB, dtype=jnp.int32)
    live_mask = jnp.concatenate([jnp.ones((PATCHES, 1), dtype=bool), slot_ids[None, :] < neighbour_count[:, None]], axis=1)
    live_mask = live_mask.reshape(device_count, P_DEV, NB + 1)

    def windows(field):
        grid = field.reshape(N_SPACE, N_SLAB, P_DEV * PT, D)
        joined = jnp.concatenate([jnp.roll(grid, 1, axis=0), grid, jnp.roll(grid, -1, axis=0)], axis=2)
        return joined.reshape(device_count, 3 * P_DEV * PT, D)

    def one_device(pieces):
        return attention(pieces[0], pieces[1], pieces[2], pieces[3], pieces[4])

    def forward(tokens, gain, query_weight, key_weight, value_weight, output_weight):
        hidden = normalize(tokens, gain)
        query = matmul(hidden, query_weight)
        key_rows = matmul(hidden, key_weight)
        value_rows = matmul(hidden, value_weight)
        mixed = lax.map(jax.checkpoint(one_device), (query.reshape(device_count, P_DEV * PT, D), windows(key_rows), windows(value_rows), block_index, live_mask))
        return matmul(mixed.reshape(TOKENS, D), output_weight) + tokens
    result, pullback = jax.vjp(forward, tokens, gain, query_weight, key_weight, value_weight, output_weight)
    d_tokens, d_gain, d_query, d_key, d_value, d_output = pullback(cotangent)
    return (result, d_tokens, d_gain, d_query, d_key, d_value, d_output)
```

```python
import jax
import jax.numpy as jnp
from jax import lax
from jax.experimental import pallas as pl
from jax.experimental.pallas import tpu as pltpu
from jax.sharding import PartitionSpec as P

MESH = pl.DeviceIdType.MESH
F32 = jnp.float32
BF16 = jnp.bfloat16
HEADS = 8
PT = 128
D = 512
HD = D // HEADS
ROWS = 256
WIN = 3 * ROWS
NX, NY, NZ = 4, 4, 8

NN = (((1,), (0,)), ((), ()))
NT = (((1,), (1,)), ((), ()))


def coords():
    s = lax.axis_index("space")
    y = lax.axis_index("slab")
    return s, s // (2 * NZ), y, (s // 2) % NZ, s % 2


def device(x, y, z, core):
    return {"space": (x * NZ + z) * 2 + core, "slab": y}


def halo_kernel(tok, left, right, send, recv):
    s = lax.axis_index("space")
    count = lax.axis_size("space")
    after = {"space": (s + 1) % count}
    before = {"space": (s + count - 1) % count}
    barrier = pltpu.get_barrier_semaphore()
    for peer in (after, before):
        pl.semaphore_signal(barrier, inc=1, device_id=peer, device_id_type=MESH)
    pl.semaphore_wait(barrier, 2)
    to_after = pltpu.make_async_remote_copy(tok, left, send.at[0], recv.at[0], device_id=after, device_id_type=MESH)
    to_before = pltpu.make_async_remote_copy(tok, right, send.at[1], recv.at[1], device_id=before, device_id_type=MESH)
    to_after.start()
    to_before.start()
    to_after.wait()
    to_before.wait()


def halo(tokens):
    shape = jax.ShapeDtypeStruct(tokens.shape, F32)
    hbm = pl.BlockSpec(memory_space=pl.ANY)
    return pl.pallas_call(
        halo_kernel,
        out_shape=(shape, shape),
        in_specs=[hbm],
        out_specs=(hbm, hbm),
        scratch_shapes=[pltpu.SemaphoreType.DMA((2,)), pltpu.SemaphoreType.DMA((2,))],
        compiler_params=pltpu.CompilerParams(collective_id=0, has_side_effects=True),
        name="halo",
    )(tokens)


def split(value):
    high = value.astype(BF16)
    return high, (value - high.astype(F32)).astype(BF16)


def dot(left, right, dims):
    return lax.dot_general(left, right, dims, preferred_element_type=F32)


def dot3(left, right, dims=NN):
    lh, ll = left
    rh, rl = right
    return dot(lh, rh, dims) + (dot(lh, rl, dims) + dot(ll, rh, dims))


def pair(ref, *index):
    return ref[(0,) + index], ref[(1,) + index]


def put(ref, value, *index):
    high, low = split(value)
    ref[(0,) + index] = high
    ref[(1,) + index] = low


ALL = slice(None)


def layer_kernel(
    nlist, ncount, tok, left, right, gain, wq, wk, wv, wo, cot,
    result, grads, dgain, dtok, dhalo,
    xhat, rstd, hid_t, k2, v2, kt2, vt2, q2, do2, do_t, o_t, dq_t, dk, dv, w2, bias,
):
    gain_row = gain[...]
    for i, ref in enumerate((left, tok, right)):
        rows = slice(i * ROWS, (i + 1) * ROWS)
        x = ref[...]
        centred = x - jnp.mean(x, axis=1, keepdims=True)
        inv = lax.rsqrt(jnp.mean(centred * centred, axis=1, keepdims=True) + 1e-5)
        xhat[rows] = centred * inv
        rstd[rows] = inv
    for i, ref in enumerate((wq, wk, wv, wo)):
        put(w2.at[i], ref[...])
    for w in range(6):
        for p in range(2):
            if w == 2 + p:
                flag = 0.0
            else:
                flag = -1e30
                for j in range(3):
                    live = jnp.logical_and(nlist[p, j] == w, j < ncount[p])
                    flag = jnp.where(live, 0.0, flag)
            bias[w * PT : (w + 1) * PT, p * PT : (p + 1) * PT] = jnp.full((PT, PT), flag, F32)
    hidden = xhat[...] * gain_row
    put(hid_t, hidden.T, ALL, ALL)
    hid2 = split(hidden)
    own2 = (hid2[0][ROWS : 2 * ROWS], hid2[1][ROWS : 2 * ROWS])
    put(q2, dot3(own2, pair(w2.at[0], ALL, ALL)), ALL, ALL)
    keys = dot3(hid2, pair(w2.at[1], ALL, ALL))
    put(k2, keys, ALL, ALL)
    put(kt2, keys.T, ALL, ALL)
    values = dot3(hid2, pair(w2.at[2], ALL, ALL))
    put(v2, values, ALL, ALL)
    put(vt2, values.T, ALL, ALL)
    cot2 = split(cot[...])
    d_mixed = dot3(cot2, pair(w2.at[3], ALL, ALL), NT)
    put(do2, d_mixed, ALL, ALL)
    do_t[...] = d_mixed.T

    @pl.loop(0, HEADS // 2)
    def _(hp):
        lanes = pl.ds(pl.multiple_of(hp * 2 * HD, 2 * HD), 2 * HD)
        q_pair, k_pair, v_pair, do_pair = (pair(ref, ALL, lanes) for ref in (q2, k2, v2, do2))
        dks, dvs = [], []
        for half in range(2):
            sl = slice(half * HD, (half + 1) * HD)
            q_h, k_h, v_h, do_h = ((a[:, sl], b[:, sl]) for a, b in (q_pair, k_pair, v_pair, do_pair))
            feats = pl.ds(pl.multiple_of(hp * 2 * HD + half * HD, HD), HD)
            scores = dot3(k_h, q_h, NT) * HD**-0.5 + bias[...]
            weights = jnp.exp(scores - jnp.max(scores, axis=0, keepdims=True))
            prob = weights * (1.0 / jnp.sum(weights, axis=0, keepdims=True))
            prob2 = split(prob)
            mixed_t = dot3(pair(vt2, feats, ALL), prob2)
            o_t[feats] = mixed_t
            dvs.append(dot3(prob2, do_h))
            d_prob = dot3(v_h, do_h, NT)
            inner = jnp.sum(mixed_t * do_t[feats], axis=0, keepdims=True)
            d_scores2 = split(prob * (d_prob - inner) * HD**-0.5)
            dq_t[feats] = dot3(pair(kt2, feats, ALL), d_scores2)
            dks.append(dot3(d_scores2, q_h))
        dk[:, lanes] = jnp.concatenate(dks, axis=1)
        dv[:, lanes] = jnp.concatenate(dvs, axis=1)

    mixed_t = o_t[...]
    grads[3] = dot3(split(mixed_t), cot2)
    result[...] = dot3(split(mixed_t.T), pair(w2.at[3], ALL, ALL)) + tok[...]
    dq_all = dq_t[...]
    own_t = pair(hid_t, ALL, slice(ROWS, 2 * ROWS))
    grads[0] = dot3(own_t, split(dq_all), NT)
    dk2 = split(dk[...])
    grads[1] = dot3(pair(hid_t, ALL, ALL), dk2)
    dv2 = split(dv[...])
    grads[2] = dot3(pair(hid_t, ALL, ALL), dv2)
    d_hidden = dot3(dk2, pair(w2.at[1], ALL, ALL), NT) + dot3(dv2, pair(w2.at[2], ALL, ALL), NT)
    dq_part = dot3(split(dq_all.T), pair(w2.at[0], ALL, ALL), NT)
    total = jnp.zeros((1, D), F32)
    for i in range(3):
        rows = slice(i * ROWS, (i + 1) * ROWS)
        part = d_hidden[rows]
        if i == 1:
            part = part + dq_part
        hat = xhat[rows]
        weighted = part * hat
        total = total + jnp.sum(weighted, axis=0, keepdims=True)
        grad = part * gain_row
        inner = jnp.mean(weighted * gain_row, axis=1, keepdims=True)
        grad = rstd[rows] * (grad - jnp.mean(grad, axis=1, keepdims=True) - hat * inner)
        if i == 1:
            dtok[...] = grad + cot[...]
        else:
            dhalo[i // 2] = grad
    dgain[...] = jnp.broadcast_to(total, dgain.shape)


def layer(nlist, ncount, tokens, left, right, gain, wq, wk, wv, wo, cot):
    vmem = pl.BlockSpec(memory_space=pltpu.VMEM)
    smem = pl.BlockSpec(memory_space=pltpu.SMEM)
    shape = jax.ShapeDtypeStruct
    return pl.pallas_call(
        layer_kernel,
        out_shape=(
            shape((ROWS, D), F32),
            shape((4, D, D), F32),
            shape((8, D), F32),
            shape((ROWS, D), F32),
            shape((2, ROWS, D), F32),
        ),
        in_specs=[smem] * 2 + [vmem] * 9,
        out_specs=(vmem,) * 5,
        scratch_shapes=[
            pltpu.VMEM((WIN, D), F32),
            pltpu.VMEM((WIN, 1), F32),
            pltpu.VMEM((2, D, WIN), BF16),
            pltpu.VMEM((2, WIN, D), BF16),
            pltpu.VMEM((2, WIN, D), BF16),
            pltpu.VMEM((2, D, WIN), BF16),
            pltpu.VMEM((2, D, WIN), BF16),
            pltpu.VMEM((2, ROWS, D), BF16),
            pltpu.VMEM((2, ROWS, D), BF16),
            pltpu.VMEM((D, ROWS), F32),
            pltpu.VMEM((D, ROWS), F32),
            pltpu.VMEM((D, ROWS), F32),
            pltpu.VMEM((WIN, D), F32),
            pltpu.VMEM((WIN, D), F32),
            pltpu.VMEM((4, 2, D, D), BF16),
            pltpu.VMEM((WIN, ROWS), F32),
        ],
        compiler_params=pltpu.CompilerParams(vmem_limit_bytes=58 << 20),
        name="layer",
    )(nlist, ncount, tokens, left, right, gain, wq, wk, wv, wo, cot)


def sum_kernel(
    grads, gain_part, dtok, dhalo,
    out, dgain, dtokens,
    own, r0, r1, acc2, r2, acc3, r3, g0, g1, g2, g3, gs, halo_in,
    send0, recv0, send1, recv1, send2, recv2, send3, recv3, send4, recv4, send5, recv5, send6, recv6, send7, recv7,
    gsend, grecv, hsend, hrecv,
):
    s, x, y, z, c = coords()
    count = lax.axis_size("space")
    partner = device(x, y, z, 1 - c)
    xs = [(x + d) % NX for d in range(NX)]
    ys = [(y + d) % NY for d in range(NY)]
    zs = [(z + d) % NZ for d in range(NZ)]
    x_peers = [device(i, y, z, c) for i in xs]
    y_peers = [device(x, i, z, c) for i in ys]
    z_peers = [device(x, y, i, c) for i in zs]
    after = {"space": (s + 1) % count, "slab": y}
    before = {"space": (s + count - 1) % count, "slab": y}
    other = {"space": (s + count - 1 + 2 * c) % count, "slab": y}
    barrier = pltpu.get_barrier_semaphore()
    everyone = [partner, other] + x_peers[1:] + y_peers[1:] + z_peers[1:]
    for peer in everyone:
        pl.semaphore_signal(barrier, inc=1, device_id=peer, device_id_type=MESH)
    pl.semaphore_wait(barrier, len(everyone))

    sent = []

    def send(src, dst, send_sem, recv_sem, peer):
        copy = pltpu.make_async_remote_copy(src, dst, send_sem, recv_sem, device_id=peer, device_id_type=MESH)
        copy.start()
        sent.append(copy)
        return copy

    orders = []
    for m in range(4):
        orders.append(((xs, x_peers), (ys, y_peers)) if m % 2 == 0 else ((ys, y_peers), (xs, x_peers)))
    mine = pl.ds(pl.multiple_of(c * 256, 128), 256)
    theirs = pl.ds(pl.multiple_of((1 - c) * 256, 128), 256)

    first = [send(grads.at[m, :, theirs], r0.at[m], send0.at[m], recv0.at[m], partner) for m in range(4)]
    gain_copies = [send(gain_part, g0, gsend.at[0], grecv.at[0], partner)]
    halo_copies = [
        send(dhalo.at[0], halo_in.at[1], hsend.at[0], hrecv.at[0], before),
        send(dhalo.at[1], halo_in.at[0], hsend.at[1], hrecv.at[1], after),
    ]
    second = []
    for m in range(4):
        first[m].wait_recv()
        own[m] = grads[m, :, mine] + r0[m]
        index, peers = orders[m][0]
        second.append(
            [
                send(
                    own.at[m, pl.ds(pl.multiple_of(index[d] * 128, 128), 128)],
                    r1.at[m, d - 1],
                    send1.at[m, d - 1],
                    recv1.at[m, d - 1],
                    peers[d],
                )
                for d in range(1, 4)
            ]
        )
    gain_copies[0].wait_recv()
    gs[0, c] = gain_part[...]
    gs[0, 1 - c] = g0[...]
    value = gs[0, 0] + gs[0, 1]
    for level, (size, peers, at, landing) in enumerate(((NX, x_peers, x, g1), (NY, y_peers, y, g2), (NZ, z_peers, z, g3))):
        gs[level + 1, at] = value
        base = (1, 4, 7)[level]
        copies = [
            send(gs.at[level + 1, at], landing.at[d - 1], gsend.at[base + d - 1], grecv.at[base + d - 1], peers[d])
            for d in range(1, size)
        ]
        for d in range(1, size):
            copies[d - 1].wait_recv()
            gs[level + 1, (at + size - d) % size] = landing[d - 1]
        value = gs[level + 1, 0]
        for i in range(1, size):
            value = value + gs[level + 1, i]
    dgain[...] = value

    third = []
    for m in range(4):
        for copy in second[m]:
            copy.wait_recv()
        at = pl.ds(pl.multiple_of(orders[m][0][0][0] * 128, 128), 128)
        acc2[m] = own[m, at] + r1[m, 0] + r1[m, 1] + r1[m, 2]
        index, peers = orders[m][1]
        third.append(
            [
                send(
                    acc2.at[m, pl.ds(pl.multiple_of(index[d] * 32, 32), 32)],
                    r2.at[m, d - 1],
                    send2.at[m, d - 1],
                    recv2.at[m, d - 1],
                    peers[d],
                )
                for d in range(1, 4)
            ]
        )

    def tile(i):
        return pl.ds(pl.multiple_of((i % 4) * 8, 8), 8), pl.ds(pl.multiple_of((i // 4) * 128, 128), 128)

    fourth = []
    for m in range(4):
        for copy in third[m]:
            copy.wait_recv()
        at = pl.ds(pl.multiple_of(orders[m][1][0][0] * 32, 32), 32)
        acc3[m] = acc2[m, at] + r2[m, 0] + r2[m, 1] + r2[m, 2]
        fourth.append(
            [
                send(acc3.at[(m,) + tile(zs[d])], r3.at[m, d - 1], send3.at[m, d - 1], recv3.at[m, d - 1], z_peers[d])
                for d in range(1, 8)
            ]
        )
    for copy in halo_copies:
        copy.wait_recv()
    dtokens[...] = dtok[...] + halo_in[0] + halo_in[1]

    def place(m, level):
        a1, a2 = orders[m][0][0][0], orders[m][1][0][0]
        if level == 0:
            return m, pl.ds(0, D), mine
        if level == 1:
            return m, pl.ds(pl.multiple_of(a1 * 128, 128), 128), mine
        row = a1 * 128 + a2 * 32
        if level == 2:
            return m, pl.ds(pl.multiple_of(row, 32), 32), mine
        return (
            m,
            pl.ds(pl.multiple_of(row + (z % 4) * 8, 8), 8),
            pl.ds(pl.multiple_of(c * 256 + (z // 4) * 128, 128), 128),
        )

    fifth = []
    for m in range(4):
        for copy in fourth[m]:
            copy.wait_recv()
        total = acc3[(m,) + tile(z)]
        for d in range(7):
            total = total + r3[m, d]
        block = place(m, 3)
        out[block] = total
        fifth.append(
            [send(out.at[block], out.at[block], send4.at[m, d - 1], recv4.at[m, d - 1], z_peers[d]) for d in range(1, 8)]
        )
    latest = fifth
    for level, (ss, rs) in enumerate(((send5, recv5), (send6, recv6), (send7, recv7))):
        copies, latest = latest, []
        for m in range(4):
            for copy in copies[m]:
                copy.wait_recv()
            block = place(m, 2 - level)
            peers = ([partner], orders[m][0][1][1:], orders[m][1][1][1:])[2 - level]
            latest.append(
                [send(out.at[block], out.at[block], ss.at[m, i], rs.at[m, i], peer) for i, peer in enumerate(peers)]
            )
    for m in range(4):
        for copy in latest[m]:
            copy.wait_recv()
    for copy in sent:
        copy.wait_send()


def sum_all(grads, gain_part, dtok, dhalo):
    vmem = pl.BlockSpec(memory_space=pltpu.VMEM)
    shape = jax.ShapeDtypeStruct
    dma = pltpu.SemaphoreType.DMA
    sems = []
    for peers in (1, 3, 3, 7, 7, 3, 3, 1):
        kind = dma((4,)) if peers == 1 and not sems else dma((4, peers))
        sems += [kind, kind]
    return pl.pallas_call(
        sum_kernel,
        out_shape=(shape((4, D, D), F32), shape((8, D), F32), shape((ROWS, D), F32)),
        in_specs=[vmem] * 4,
        out_specs=(vmem,) * 3,
        scratch_shapes=[
            pltpu.VMEM((4, D, 256), F32),
            pltpu.VMEM((4, D, 256), F32),
            pltpu.VMEM((4, 3, 128, 256), F32),
            pltpu.VMEM((4, 128, 256), F32),
            pltpu.VMEM((4, 3, 32, 256), F32),
            pltpu.VMEM((4, 32, 256), F32),
            pltpu.VMEM((4, 7, 8, 128), F32),
            pltpu.VMEM((8, D), F32),
            pltpu.VMEM((3, 8, D), F32),
            pltpu.VMEM((3, 8, D), F32),
            pltpu.VMEM((7, 8, D), F32),
            pltpu.VMEM((4, 8, 8, D), F32),
            pltpu.VMEM((2, ROWS, D), F32),
        ]
        + sems
        + [dma((14,)), dma((14,)), dma((2,)), dma((2,))],
        compiler_params=pltpu.CompilerParams(
            collective_id=1, has_side_effects=True, vmem_limit_bytes=48 << 20
        ),
        name="sum_all",
    )(grads, gain_part, dtok, dhalo)


def body(tokens, gain, wq, wk, wv, wo, nlist, ncount, cot):
    left, right = halo(tokens)
    result, grads, gain_part, dtok, dhalo = layer(
        nlist, ncount, tokens, left, right, gain[None, :], wq, wk, wv, wo, cot
    )
    sums, gain_sum, d_tokens = sum_all(grads, gain_part, dtok, dhalo)
    return (result, d_tokens, gain_sum[0], sums[0], sums[1], sums[2], sums[3])


def solution(mesh):
    rows = P(("space", "slab"), None)
    return jax.shard_map(
        body,
        mesh=mesh,
        in_specs=(rows, P(), P(), P(), P(), P(), rows, P(("space", "slab")), rows),
        out_specs=(rows, rows, P(), P(), P(), P(), P()),
        check_vma=False,
    )
```

```python
import jax
import jax.numpy as jnp
from jax import lax
from jax.experimental import pallas as pl
from jax.experimental.pallas import tpu as pltpu
from jax.sharding import PartitionSpec as P

MESH = pl.DeviceIdType.MESH
F32 = jnp.float32
BF16 = jnp.bfloat16
HEADS = 8
PT = 128
D = 512
HD = D // HEADS
ROWS = 256
WIN = 3 * ROWS
NX, NY, NZ = 4, 4, 8
QUARTERS = 4
LANES = 128

NN = (((1,), (0,)), ((), ()))
NT = (((1,), (1,)), ((), ()))


def device(x, y, z, core):
    return {"space": (x * NZ + z) * 2 + core, "slab": y}


def split(value):
    high = value.astype(BF16)
    return high, (value - high.astype(F32)).astype(BF16)


def dot(left, right, dims=NN):
    return lax.dot_general(left, right, dims, preferred_element_type=F32)


def dot3(left, right, dims=NN):
    lh, ll = left
    rh, rl = right
    return dot(lh, rh, dims) + (dot(lh, rl, dims) + dot(ll, rh, dims))


def pair(ref, *index):
    return ref[(0,) + index], ref[(1,) + index]


def put(ref, value, *index):
    high, low = split(value)
    ref[(0,) + index] = high
    ref[(1,) + index] = low
    return high, low


ALL = slice(None)


def at(start, size, step=None):
    return pl.ds(pl.multiple_of(start, step or size), size)


def packed(value):
    high = value.astype(BF16).astype(F32)
    low = value - high
    first = lax.broadcasted_iota(jnp.int32, value.shape, 1) < HD
    high_r, low_r = pltpu.roll(high, HD, 1), pltpu.roll(low, HD, 1)
    hl = (jnp.where(first, high, low_r).astype(BF16), jnp.where(first, high_r, low).astype(BF16))
    lh = (jnp.where(first, low, high_r).astype(BF16), jnp.where(first, low_r, high).astype(BF16))
    return hl, lh


def kernel(
    nlist, ncount, tok, gain, wq, wk, wv, wo, cot,
    result, d_tokens, d_gain, d_q, d_k, d_v, d_o,
    xwin, wf, cotf, xhat, rstd, hid_t, w2, cot2, kp, vp, kt, vt, qp, dop, do_t, bias, dk2, dv2, dq2, o2,
    g, r0, r1, acc2, r2, acc3, r3, full, dhalo, halo_in, res_buf, dtok_buf, dg_acc,
    load_sem, tok_send, tok_recv, s0, q0, s1, q1, s2, q2, s3, q3, s4, q4, s5, q5, s6, q6, s7, q7,
    dh_send, dh_recv, out_sem,
):
    s = lax.axis_index("space")
    y = lax.axis_index("slab")
    count = NX * NZ * 2
    x, z, c = s // (2 * NZ), (s // 2) % NZ, s % 2
    partner = device(x, y, z, 1 - c)
    after = {"space": (s + 1) % count, "slab": y}
    before = {"space": (s + count - 1) % count, "slab": y}
    other = {"space": (s + count - 1 + 2 * c) % count, "slab": y}

    loads = [pltpu.make_async_copy(tok, xwin.at[pl.ds(ROWS, ROWS)], load_sem.at[0])]
    for i, ref in enumerate((wq, wk, wv, wo)):
        loads.append(pltpu.make_async_copy(ref, wf.at[i], load_sem.at[1 + i]))
    loads.append(pltpu.make_async_copy(cot, cotf, load_sem.at[5]))
    for load in loads:
        load.start()

    barrier = pltpu.get_barrier_semaphore()
    everyone = [partner, other]
    everyone += [device((x + d) % NX, y, z, c) for d in range(1, NX)]
    everyone += [device(x, (y + d) % NY, z, c) for d in range(1, NY)]
    everyone += [device(x, y, (z + d) % NZ, c) for d in range(1, NZ)]
    for peer in everyone:
        pl.semaphore_signal(barrier, inc=1, device_id=peer, device_id_type=MESH)
    pl.semaphore_wait(barrier, len(everyone))

    def remote(src, dst, send_sem, recv_sem, peer):
        return pltpu.make_async_remote_copy(src, dst, send_sem, recv_sem, device_id=peer, device_id_type=MESH)

    to_after = remote(tok, xwin.at[pl.ds(0, ROWS)], tok_send.at[0], tok_recv.at[0], after)
    to_before = remote(tok, xwin.at[pl.ds(2 * ROWS, ROWS)], tok_send.at[1], tok_recv.at[1], before)
    to_after.start()
    to_before.start()

    gain_row = gain[...]
    for w in range(6):
        for p in range(2):
            if w == 2 + p:
                flag = 0.0
            else:
                flag = -1e30
                for j in range(3):
                    live = jnp.logical_and(nlist[p, j] == w, j < ncount[p])
                    flag = jnp.where(live, 0.0, flag)
            bias[w * PT : (w + 1) * PT, p * PT : (p + 1) * PT] = jnp.full((PT, PT), flag, F32)

    def keys_values(block):
        rows = slice(block * ROWS, (block + 1) * ROWS)
        tokens = xwin[rows]
        centred = tokens - jnp.mean(tokens, axis=1, keepdims=True)
        inv = lax.rsqrt(jnp.mean(centred * centred, axis=1, keepdims=True) + 1e-5)
        hat = centred * inv
        xhat[rows] = hat
        rstd[rows] = inv
        hidden = hat * gain_row
        put(hid_t, hidden.T, ALL, rows)
        hidden2 = split(hidden)
        for i, pack, turned in ((1, kp, kt), (2, vp, vt)):
            value = dot3(hidden2, pair(w2.at[i], ALL, ALL))
            for hp in range(HEADS // 2):
                hl, _ = packed(value[:, hp * LANES : (hp + 1) * LANES])
                for half in range(2):
                    h = 2 * hp + half
                    pack[rows, h * LANES : (h + 1) * LANES] = hl[half]
            high, low = split(value.T)
            for h in range(HEADS):
                turned[h * LANES : h * LANES + HD, rows] = high[h * HD : (h + 1) * HD]
                turned[h * LANES + HD : (h + 1) * LANES, rows] = low[h * HD : (h + 1) * HD]
        return hidden2

    def pack_rows(pack, value):
        for hp in range(HEADS // 2):
            hl, lh = packed(value[:, hp * LANES : (hp + 1) * LANES])
            for half in range(2):
                h = 2 * hp + half
                pack[:, h * 2 * LANES : h * 2 * LANES + LANES] = hl[half]
                pack[:, h * 2 * LANES + LANES : (h + 1) * 2 * LANES] = lh[half]

    loads[0].wait()
    loads[2].wait()
    put(w2.at[1], wf[1], ALL, ALL)
    loads[3].wait()
    put(w2.at[2], wf[2], ALL, ALL)
    hidden2 = keys_values(1)
    loads[1].wait()
    put(w2.at[0], wf[0], ALL, ALL)
    pack_rows(qp, dot3(hidden2, pair(w2.at[0], ALL, ALL)) * HD**-0.5)
    loads[4].wait()
    put(w2.at[3], wf[3], ALL, ALL)
    loads[5].wait()
    put(cot2, cotf[...], ALL, ALL)
    d_mixed = dot3(pair(cot2, ALL, ALL), pair(w2.at[3], ALL, ALL), NT)
    pack_rows(dop, d_mixed)
    do_t[...] = d_mixed.T
    to_after.wait_recv()
    keys_values(0)
    to_before.wait_recv()
    keys_values(2)

    def axes(q):
        odd = q % 2
        even = 1 - odd
        one = x * even + y * odd
        two = x * odd + y * even

        def along_one(d):
            return device((x + d * even) % NX, (y + d * odd) % NY, z, c)

        def along_two(d):
            return device((x + d * odd) % NX, (y + d * even) % NY, z, c)

        return one, two, along_one, along_two

    def along_z(d):
        return device(x, y, (z + d) % NZ, c)

    def copies(level, q):
        one, two, along_one, along_two = axes(q)
        base1 = c * 1024 + one * 256
        base2 = base1 + two * 64
        if level == 0:
            return [remote(g.at[q, at((1 - c) * 1024, 1024)], r0.at[q], s0.at[q], q0.at[q], partner)]
        if level == 1:
            return [
                remote(
                    g.at[q, at(c * 1024 + ((one + d) % 4) * 256, 256)],
                    r1.at[q, d - 1], s1.at[q, d - 1], q1.at[q, d - 1], along_one(d),
                )
                for d in range(1, 4)
            ]
        if level == 2:
            return [
                remote(
                    acc2.at[q, at(((two + d) % 4) * 64, 64)],
                    r2.at[q, d - 1], s2.at[q, d - 1], q2.at[q, d - 1], along_two(d),
                )
                for d in range(1, 4)
            ]
        if level == 3:
            return [
                remote(
                    acc3.at[q, at(((z + d) % NZ) * 8, 8)],
                    r3.at[q, d - 1], s3.at[q, d - 1], q3.at[q, d - 1], along_z(d),
                )
                for d in range(1, 8)
            ]
        if level == 4:
            block = full.at[q, at(base2 + z * 8, 8)]
            return [remote(block, block, s4.at[q, d - 1], q4.at[q, d - 1], along_z(d)) for d in range(1, 8)]
        if level == 5:
            block = full.at[q, at(base2, 64)]
            return [remote(block, block, s5.at[q, d - 1], q5.at[q, d - 1], along_two(d)) for d in range(1, 4)]
        if level == 6:
            block = full.at[q, at(base1, 256)]
            return [remote(block, block, s6.at[q, d - 1], q6.at[q, d - 1], along_one(d)) for d in range(1, 4)]
        block = full.at[q, at(c * 1024, 1024)]
        return [remote(block, block, s7.at[q], q7.at[q], partner)]

    def go(level, q):
        for copy in copies(level, q):
            copy.start()

    def arrived(level, q):
        for copy in copies(level, q):
            copy.wait_recv()

    def step(level, q):
        one, two, _, _ = axes(q)
        base1 = c * 1024 + one * 256
        arrived(level - 1, q)
        if level == 1:
            mine = at(c * 1024, 1024)
            g[q, mine] = g[q, mine] + r0[q]
        elif level == 2:
            acc2[q] = (g[q, at(base1, 256)] + r1[q, 0]) + (r1[q, 1] + r1[q, 2])
        elif level == 3:
            acc3[q] = (acc2[q, at(two * 64, 64)] + r2[q, 0]) + (r2[q, 1] + r2[q, 2])
        elif level == 4:
            total = acc3[q, at(z * 8, 8)]
            for d in range(7):
                total = total + r3[q, d]
            full[q, at(base1 + two * 64 + z * 8, 8)] = total
        go(level, q)

    @pl.loop(0, QUARTERS)
    def _(hp):
        lanes = at(hp * LANES, LANES)
        first = lax.broadcasted_iota(jnp.int32, (WIN, LANES), 1) < HD
        sums_k, sums_v, mixed_ts, dq_ts = [], [], [], []
        for half in range(2):
            h = hp * 2 + half
            own = at(h * LANES, LANES)
            double = at(h * 2 * LANES, 2 * LANES)
            k_h, v_h = kp[:, own], vp[:, own]
            q_h, do_h = qp[:, double], dop[:, double]
            scores = dot(jnp.concatenate([k_h, k_h], axis=1), q_h, NT) + bias[...]
            weights = jnp.exp(scores - jnp.max(scores, axis=0, keepdims=True))
            prob = weights * (1.0 / jnp.sum(weights, axis=0, keepdims=True))
            p_high, p_low = split(prob)
            v_t = vt[own]
            both = dot(v_t, p_high) + dot(v_t, p_low)
            mixed_t = both[:HD] + both[HD:]
            mixed_ts.append(mixed_t)
            do_hl = do_h[:, :LANES]
            sum_v = dot(p_high, do_hl) + dot(p_low, do_hl)
            sums_v.append(sum_v + pltpu.roll(sum_v, HD, 1))
            d_prob = dot(jnp.concatenate([v_h, v_h], axis=1), do_h, NT)
            inner = jnp.sum(mixed_t * do_t[at(h * HD, HD)], axis=0, keepdims=True)
            ds_high, ds_low = split(prob * (d_prob - inner))
            k_t = kt[own]
            both = dot(k_t, ds_high) + dot(k_t, ds_low)
            dq_ts.append((both[:HD] + both[HD:]) * HD**-0.5)
            q_hl = q_h[:, :LANES]
            sum_k = dot(ds_high, q_hl) + dot(ds_low, q_hl)
            sums_k.append(sum_k + pltpu.roll(sum_k, HD, 1))
        dk_pair = put(dk2, jnp.where(first, sums_k[0], sums_k[1]), ALL, lanes)
        dv_pair = put(dv2, jnp.where(first, sums_v[0], sums_v[1]), ALL, lanes)
        dq_pair = put(dq2, jnp.concatenate(dq_ts, axis=0).T, ALL, lanes)
        mixed_t = jnp.concatenate(mixed_ts, axis=0)
        put(o2, mixed_t.T, ALL, lanes)
        kv = tuple(jnp.concatenate([a, b], axis=1) for a, b in zip(dk_pair, dv_pair))
        grad_kv = dot3(pair(hid_t, ALL, ALL), kv)
        g[hp, :D] = dot3(pair(hid_t, ALL, slice(ROWS, 2 * ROWS)), dq_pair)
        g[hp, D : 2 * D] = grad_kv[:, :LANES]
        g[hp, 2 * D : 3 * D] = grad_kv[:, LANES:]
        grad_o = dot3(split(mixed_t), pair(cot2, ALL, ALL))
        for i in range(4):
            g[hp, 3 * D + i * LANES : 3 * D + (i + 1) * LANES] = grad_o[:, i * LANES : (i + 1) * LANES]
        go(0, hp)
        for level in range(1, 4):

            @pl.when(hp >= level)
            def _(level=level):
                step(level, hp - level)

    def d_hidden(block):
        rows = slice(block * ROWS, (block + 1) * ROWS)
        part = dot3(pair(dk2, rows, ALL), pair(w2.at[1], ALL, ALL), NT)
        part = part + dot3(pair(dv2, rows, ALL), pair(w2.at[2], ALL, ALL), NT)
        if block == 1:
            part = part + dot3(pair(dq2, ALL, ALL), pair(w2.at[0], ALL, ALL), NT)
        grad = part * gain_row
        hat = xhat[rows]
        inner = jnp.mean(grad * hat, axis=1, keepdims=True)
        return rstd[rows] * (grad - jnp.mean(grad, axis=1, keepdims=True) - hat * inner)

    back = [
        remote(dhalo.at[0], halo_in.at[1], dh_send.at[0], dh_recv.at[0], before),
        remote(dhalo.at[1], halo_in.at[0], dh_send.at[1], dh_recv.at[1], after),
    ]
    outs = []

    def write(src, dst, sem):
        copy = pltpu.make_async_copy(src, dst, sem)
        copy.start()
        outs.append(copy)

    dhalo[0] = d_hidden(0)
    back[0].start()
    step(1, 3)
    step(2, 2)
    step(3, 1)
    step(4, 0)
    dhalo[1] = d_hidden(2)
    back[1].start()
    step(4, 1)
    step(3, 2)
    step(2, 3)
    step(5, 0)
    dtok_buf[...] = d_hidden(1) + cotf[...]
    step(4, 2)
    step(5, 1)
    step(3, 3)
    step(6, 0)
    res_buf[...] = dot3(pair(o2, ALL, ALL), pair(w2.at[3], ALL, ALL)) + xwin[ROWS : 2 * ROWS]
    write(res_buf, result, out_sem.at[0])
    step(5, 2)
    step(6, 1)
    step(4, 3)
    step(7, 0)
    step(6, 2)
    step(5, 3)
    step(7, 1)
    for copy in back:
        copy.wait_recv()
    dtok_buf[...] = dtok_buf[...] + (halo_in[0] + halo_in[1])
    write(dtok_buf, d_tokens, out_sem.at[1])
    dg_acc[...] = jnp.zeros_like(dg_acc)

    def finish(q):
        arrived(7, q)
        lanes = slice(q * LANES, (q + 1) * LANES)
        for i, ref in enumerate((d_q, d_k, d_v)):
            write(full.at[q, pl.ds(i * D, D)], ref.at[:, pl.ds(q * LANES, LANES)], out_sem.at[2 + q * 7 + i])
        for i in range(4):
            write(
                full.at[q, pl.ds(3 * D + i * LANES, LANES)],
                d_o.at[pl.ds(q * LANES, LANES), pl.ds(i * LANES, LANES)],
                out_sem.at[2 + q * 7 + 3 + i],
            )
        dg_acc[...] += (
            full[q, :D] * wf[0, :, lanes] + full[q, D : 2 * D] * wf[1, :, lanes] + full[q, 2 * D : 3 * D] * wf[2, :, lanes]
        )

    finish(0)
    step(6, 3)
    step(7, 2)
    finish(1)
    finish(2)
    step(7, 3)
    finish(3)
    d_gain[...] = jnp.broadcast_to(jnp.sum(dg_acc[...].T, axis=0, keepdims=True) / gain_row, d_gain.shape)
    to_after.wait_send()
    to_before.wait_send()
    for copy in back:
        copy.wait_send()
    for q in range(QUARTERS):
        for level in range(8):
            for copy in copies(level, q):
                copy.wait_send()
    for copy in outs:
        copy.wait()


def layer(nlist, ncount, tokens, gain, wq, wk, wv, wo, cot):
    vmem = pl.BlockSpec(memory_space=pltpu.VMEM)
    smem = pl.BlockSpec(memory_space=pltpu.SMEM)
    hbm = pl.BlockSpec(memory_space=pl.ANY)
    shape = jax.ShapeDtypeStruct
    dma = pltpu.SemaphoreType.DMA
    v = pltpu.VMEM
    wide = HEADS * LANES
    scratch = [
        v((WIN, D), F32),
        v((4, D, D), F32),
        v((ROWS, D), F32),
        v((WIN, D), F32),
        v((WIN, 1), F32),
        v((2, D, WIN), BF16),
        v((4, 2, D, D), BF16),
        v((2, ROWS, D), BF16),
        v((WIN, wide), BF16),
        v((WIN, wide), BF16),
        v((wide, WIN), BF16),
        v((wide, WIN), BF16),
        v((ROWS, 2 * wide), BF16),
        v((ROWS, 2 * wide), BF16),
        v((D, ROWS), F32),
        v((WIN, ROWS), F32),
        v((2, WIN, D), BF16),
        v((2, WIN, D), BF16),
        v((2, ROWS, D), BF16),
        v((2, ROWS, D), BF16),
        v((4, 2048, LANES), F32),
        v((4, 1024, LANES), F32),
        v((4, 3, 256, LANES), F32),
        v((4, 256, LANES), F32),
        v((4, 3, 64, LANES), F32),
        v((4, 64, LANES), F32),
        v((4, 7, 8, LANES), F32),
        v((4, 2048, LANES), F32),
        v((2, ROWS, D), F32),
        v((2, ROWS, D), F32),
        v((ROWS, D), F32),
        v((ROWS, D), F32),
        v((D, LANES), F32),
        dma((6,)),
        dma((2,)),
        dma((2,)),
    ]
    for peers in ((4,), (4, 3), (4, 3), (4, 7), (4, 7), (4, 3), (4, 3), (4,)):
        scratch += [dma(peers), dma(peers)]
    scratch += [dma((2,)), dma((2,)), dma((30,))]
    return pl.pallas_call(
        kernel,
        out_shape=(
            shape((ROWS, D), F32),
            shape((ROWS, D), F32),
            shape((8, D), F32),
            shape((D, D), F32),
            shape((D, D), F32),
            shape((D, D), F32),
            shape((D, D), F32),
        ),
        in_specs=[smem] * 2 + [hbm, vmem] + [hbm] * 5,
        out_specs=(hbm, hbm, vmem, hbm, hbm, hbm, hbm),
        scratch_shapes=scratch,
        compiler_params=pltpu.CompilerParams(
            collective_id=0, has_side_effects=True, vmem_limit_bytes=60 << 20
        ),
        name="patch_layer",
    )(nlist, ncount, tokens, gain, wq, wk, wv, wo, cot)


def body(tokens, gain, wq, wk, wv, wo, nlist, ncount, cot):
    result, d_tokens, d_gain, d_q, d_k, d_v, d_o = layer(
        nlist, ncount, tokens, gain[None, :], wq, wk, wv, wo, cot
    )
    return (result, d_tokens, d_gain[0], d_q, d_k, d_v, d_o)


def solution(mesh):
    rows = P(("space", "slab"), None)
    return jax.shard_map(
        body,
        mesh=mesh,
        in_specs=(rows, P(), P(), P(), P(), P(), rows, P(("space", "slab")), rows),
        out_specs=(rows, rows, P(), P(), P(), P(), P()),
        check_vma=False,
    )
```

```python
import jax
import jax.numpy as jnp
from jax import lax
from jax.experimental import pallas as pl
from jax.experimental.pallas import tpu as pltpu
from jax.sharding import PartitionSpec as P

MESH = pl.DeviceIdType.MESH
F32 = jnp.float32
BF16 = jnp.bfloat16
HEADS = 8
PT = 128
D = 512
HD = D // HEADS
ROWS = 256
WIN = 3 * ROWS
NX, NY, NZ = 4, 4, 8
QUARTERS = 4
LANES = 128

NN = (((1,), (0,)), ((), ()))
NT = (((1,), (1,)), ((), ()))


def device(x, y, z, core):
    return {"space": (x * NZ + z) * 2 + core, "slab": y}


def split(value):
    high = value.astype(BF16)
    return high, (value - high.astype(F32)).astype(BF16)


def dot(left, right, dims=NN):
    return lax.dot_general(left, right, dims, preferred_element_type=F32)


def dot3(left, right, dims=NN):
    lh, ll = left
    rh, rl = right
    return dot(lh, rh, dims) + (dot(lh, rl, dims) + dot(ll, rh, dims))


def pair(ref, *index):
    return ref[(0,) + index], ref[(1,) + index]


def put(ref, value, *index):
    high, low = split(value)
    ref[(0,) + index] = high
    ref[(1,) + index] = low
    return high, low


ALL = slice(None)


def at(start, size, step=None):
    return pl.ds(pl.multiple_of(start, step or size), size)


def packed(value):
    high = value.astype(BF16).astype(F32)
    low = value - high
    first = lax.broadcasted_iota(jnp.int32, value.shape, 1) < HD
    high_r, low_r = pltpu.roll(high, HD, 1), pltpu.roll(low, HD, 1)
    hl = (jnp.where(first, high, low_r).astype(BF16), jnp.where(first, high_r, low).astype(BF16))
    lh = (jnp.where(first, low, high_r).astype(BF16), jnp.where(first, low_r, high).astype(BF16))
    return hl, lh


def kernel(
    nlist, ncount, tok, gain, wq, wk, wv, wo, cot,
    result, d_tokens, d_gain, d_q, d_k, d_v, d_o,
    xwin, wf, cotf, xhat, rstd, hid_t, w2, cot2, kp, vp, kt, vt, qp, dop, do_t, bias, dk2, dv2, dq2, o2,
    g, r0, r1, acc2, r2, acc3, r3, full, dhalo, halo_in, res_buf, dtok_buf, dg_acc,
    load_sem, tok_send, tok_recv, s0, q0, s1, q1, s2, q2, s3, q3, s4, q4, s5, q5, s6, q6, s7, q7,
    dh_send, dh_recv, out_sem,
):
    s = lax.axis_index("space")
    y = lax.axis_index("slab")
    count = NX * NZ * 2
    x, z, c = s // (2 * NZ), (s // 2) % NZ, s % 2
    partner = device(x, y, z, 1 - c)
    after = {"space": (s + 1) % count, "slab": y}
    before = {"space": (s + count - 1) % count, "slab": y}
    other = {"space": (s + count - 1 + 2 * c) % count, "slab": y}

    loads = [pltpu.make_async_copy(tok, xwin.at[pl.ds(ROWS, ROWS)], load_sem.at[0])]
    for i, ref in enumerate((wq, wk, wv, wo)):
        loads.append(pltpu.make_async_copy(ref, wf.at[i], load_sem.at[1 + i]))
    loads.append(pltpu.make_async_copy(cot, cotf, load_sem.at[5]))
    for load in loads:
        load.start()

    barrier = pltpu.get_barrier_semaphore()
    everyone = [partner, other]
    everyone += [device((x + d) % NX, y, z, c) for d in range(1, NX)]
    everyone += [device(x, (y + d) % NY, z, c) for d in range(1, NY)]
    everyone += [device(x, y, (z + d) % NZ, c) for d in range(1, NZ)]
    for peer in everyone:
        pl.semaphore_signal(barrier, inc=1, device_id=peer, device_id_type=MESH)
    pl.semaphore_wait(barrier, len(everyone))

    def remote(src, dst, send_sem, recv_sem, peer):
        return pltpu.make_async_remote_copy(src, dst, send_sem, recv_sem, device_id=peer, device_id_type=MESH)

    to_after = remote(tok, xwin.at[pl.ds(0, ROWS)], tok_send.at[0], tok_recv.at[0], after)
    to_before = remote(tok, xwin.at[pl.ds(2 * ROWS, ROWS)], tok_send.at[1], tok_recv.at[1], before)
    to_after.start()
    to_before.start()

    gain_row = gain[...]
    for w in range(6):
        for p in range(2):
            if w == 2 + p:
                flag = 0.0
            else:
                flag = -1e30
                for j in range(3):
                    live = jnp.logical_and(nlist[p, j] == w, j < ncount[p])
                    flag = jnp.where(live, 0.0, flag)
            bias[w * PT : (w + 1) * PT, p * PT : (p + 1) * PT] = jnp.full((PT, PT), flag, F32)

    def keys_values(block):
        rows = slice(block * ROWS, (block + 1) * ROWS)
        tokens = xwin[rows]
        centred = tokens - jnp.mean(tokens, axis=1, keepdims=True)
        inv = lax.rsqrt(jnp.mean(centred * centred, axis=1, keepdims=True) + 1e-5)
        hat = centred * inv
        xhat[rows] = hat
        rstd[rows] = inv
        hidden = hat * gain_row
        put(hid_t, hidden.T, ALL, rows)
        hidden2 = split(hidden)
        for i, pack, turned in ((1, kp, kt), (2, vp, vt)):
            value = dot3(hidden2, pair(w2.at[i], ALL, ALL))
            for hp in range(HEADS // 2):
                hl, _ = packed(value[:, hp * LANES : (hp + 1) * LANES])
                for half in range(2):
                    h = 2 * hp + half
                    pack[rows, h * LANES : (h + 1) * LANES] = hl[half]
            high, low = split(value.T)
            for h in range(HEADS):
                turned[h * LANES : h * LANES + HD, rows] = high[h * HD : (h + 1) * HD]
                turned[h * LANES + HD : (h + 1) * LANES, rows] = low[h * HD : (h + 1) * HD]
        return hidden2

    def pack_rows(pack, value):
        for hp in range(HEADS // 2):
            hl, lh = packed(value[:, hp * LANES : (hp + 1) * LANES])
            for half in range(2):
                h = 2 * hp + half
                pack[:, h * 2 * LANES : h * 2 * LANES + LANES] = hl[half]
                pack[:, h * 2 * LANES + LANES : (h + 1) * 2 * LANES] = lh[half]

    loads[0].wait()
    loads[2].wait()
    put(w2.at[1], wf[1], ALL, ALL)
    loads[3].wait()
    put(w2.at[2], wf[2], ALL, ALL)
    hidden2 = keys_values(1)
    loads[1].wait()
    put(w2.at[0], wf[0], ALL, ALL)
    pack_rows(qp, dot3(hidden2, pair(w2.at[0], ALL, ALL)) * HD**-0.5)
    loads[4].wait()
    put(w2.at[3], wf[3], ALL, ALL)
    loads[5].wait()
    put(cot2, cotf[...], ALL, ALL)
    d_mixed = dot3(pair(cot2, ALL, ALL), pair(w2.at[3], ALL, ALL), NT)
    pack_rows(dop, d_mixed)
    do_t[...] = d_mixed.T
    to_after.wait_recv()
    keys_values(0)
    to_before.wait_recv()
    keys_values(2)

    half_a = c * 1024
    half_b = half_a + 512
    x_rows, y_rows = half_a + x * 128, half_b + y * 128
    xy_rows, yx_rows = x_rows + y * 32, y_rows + x * 32
    upper = z // 4
    tile = xy_rows * (1 - upper) + yx_rows * upper + (z % 4) * 8

    def along_x(d):
        return device((x + d) % NX, y, z, c)

    def along_y(d):
        return device(x, (y + d) % NY, z, c)

    def along_z(d):
        return device(x, y, (z + d) % NZ, c)

    def copies(level, q):
        if level == 0:
            return [remote(g.at[q, at((1 - c) * 1024, 1024)], r0.at[q], s0.at[q], q0.at[q], partner)]
        if level == 7:
            block = full.at[q, at(c * 1024, 1024)]
            return [remote(block, block, s7.at[q], q7.at[q], partner)]
        if level == 3:
            return [
                remote(acc3.at[q, at(((z + d) % NZ) * 8, 8)], r3.at[q, d - 1], s3.at[q, d - 1], q3.at[q, d - 1], along_z(d))
                for d in range(1, NZ)
            ]
        if level == 4:
            block = full.at[q, at(tile, 8)]
            return [remote(block, block, s4.at[q, d - 1], q4.at[q, d - 1], along_z(d)) for d in range(1, NZ)]
        found = []
        for d in range(1, 4):
            xd, yd = (x + d) % NX, (y + d) % NY
            if level == 1:
                a = (g.at[q, at(half_a + xd * 128, 128)], r1.at[q, 0, d - 1], along_x(d))
                b = (g.at[q, at(half_b + yd * 128, 128)], r1.at[q, 1, d - 1], along_y(d))
                ss, rs = s1, q1
            elif level == 2:
                a = (acc2.at[q, 0, at(yd * 32, 32)], r2.at[q, 0, d - 1], along_y(d))
                b = (acc2.at[q, 1, at(xd * 32, 32)], r2.at[q, 1, d - 1], along_x(d))
                ss, rs = s2, q2
            elif level == 5:
                a = (full.at[q, at(xy_rows, 32)], full.at[q, at(xy_rows, 32)], along_y(d))
                b = (full.at[q, at(yx_rows, 32)], full.at[q, at(yx_rows, 32)], along_x(d))
                ss, rs = s5, q5
            else:
                a = (full.at[q, at(x_rows, 128)], full.at[q, at(x_rows, 128)], along_x(d))
                b = (full.at[q, at(y_rows, 128)], full.at[q, at(y_rows, 128)], along_y(d))
                ss, rs = s6, q6
            for i, (src, dst, peer) in enumerate((a, b)):
                found.append(remote(src, dst, ss.at[q, i * 3 + d - 1], rs.at[q, i * 3 + d - 1], peer))
        return found

    def go(level, q):
        for copy in copies(level, q):
            copy.start()

    def arrived(level, q):
        for copy in copies(level, q):
            copy.wait_recv()

    def step(level, q):
        arrived(level - 1, q)
        if level == 1:
            mine = at(c * 1024, 1024)
            g[q, mine] = g[q, mine] + r0[q]
        elif level == 2:
            for i, rows in enumerate((x_rows, y_rows)):
                acc2[q, i] = (g[q, at(rows, 128)] + r1[q, i, 0]) + (r1[q, i, 1] + r1[q, i, 2])
        elif level == 3:
            for i, row in enumerate((y * 32, x * 32)):
                acc3[q, i * 32 : i * 32 + 32] = (acc2[q, i, at(row, 32)] + r2[q, i, 0]) + (r2[q, i, 1] + r2[q, i, 2])
        elif level == 4:
            total = acc3[q, at(z * 8, 8)]
            for d in range(7):
                total = total + r3[q, d]
            full[q, at(tile, 8)] = total
        go(level, q)

    @pl.loop(0, QUARTERS)
    def _(hp):
        lanes = at(hp * LANES, LANES)
        first = lax.broadcasted_iota(jnp.int32, (WIN, LANES), 1) < HD
        sums_k, sums_v, mixed_ts, dq_ts = [], [], [], []
        for half in range(2):
            h = hp * 2 + half
            own = at(h * LANES, LANES)
            double = at(h * 2 * LANES, 2 * LANES)
            k_h, v_h = kp[:, own], vp[:, own]
            q_h, do_h = qp[:, double], dop[:, double]
            scores = dot(jnp.concatenate([k_h, k_h], axis=1), q_h, NT) + bias[...]
            weights = jnp.exp(scores - jnp.max(scores, axis=0, keepdims=True))
            prob = weights * (1.0 / jnp.sum(weights, axis=0, keepdims=True))
            p_high, p_low = split(prob)
            v_t = vt[own]
            both = dot(v_t, p_high) + dot(v_t, p_low)
            mixed_t = both[:HD] + both[HD:]
            mixed_ts.append(mixed_t)
            do_hl = do_h[:, :LANES]
            sum_v = dot(p_high, do_hl) + dot(p_low, do_hl)
            sums_v.append(sum_v + pltpu.roll(sum_v, HD, 1))
            d_prob = dot(jnp.concatenate([v_h, v_h], axis=1), do_h, NT)
            inner = jnp.sum(mixed_t * do_t[at(h * HD, HD)], axis=0, keepdims=True)
            ds_high, ds_low = split(prob * (d_prob - inner))
            k_t = kt[own]
            both = dot(k_t, ds_high) + dot(k_t, ds_low)
            dq_ts.append((both[:HD] + both[HD:]) * HD**-0.5)
            q_hl = q_h[:, :LANES]
            sum_k = dot(ds_high, q_hl) + dot(ds_low, q_hl)
            sums_k.append(sum_k + pltpu.roll(sum_k, HD, 1))
            if half == 0:

                @pl.when(hp >= 1)
                def _():
                    step(1, hp - 1)

        dk_pair = put(dk2, jnp.where(first, sums_k[0], sums_k[1]), ALL, lanes)
        dv_pair = put(dv2, jnp.where(first, sums_v[0], sums_v[1]), ALL, lanes)
        dq_pair = put(dq2, jnp.concatenate(dq_ts, axis=0).T, ALL, lanes)
        mixed_t = jnp.concatenate(mixed_ts, axis=0)
        put(o2, mixed_t.T, ALL, lanes)
        kv = tuple(jnp.concatenate([a, b], axis=1) for a, b in zip(dk_pair, dv_pair))
        grad_kv = dot3(pair(hid_t, ALL, ALL), kv)
        g[hp, :D] = dot3(pair(hid_t, ALL, slice(ROWS, 2 * ROWS)), dq_pair)
        g[hp, D : 2 * D] = grad_kv[:, :LANES]
        g[hp, 2 * D : 3 * D] = grad_kv[:, LANES:]
        grad_o = dot3(split(mixed_t), pair(cot2, ALL, ALL))
        for i in range(4):
            g[hp, 3 * D + i * LANES : 3 * D + (i + 1) * LANES] = grad_o[:, i * LANES : (i + 1) * LANES]
        go(0, hp)
        for level in range(2, 4):

            @pl.when(hp >= level)
            def _(level=level):
                step(level, hp - level)

    def d_hidden(block):
        rows = slice(block * ROWS, (block + 1) * ROWS)
        part = dot3(pair(dk2, rows, ALL), pair(w2.at[1], ALL, ALL), NT)
        part = part + dot3(pair(dv2, rows, ALL), pair(w2.at[2], ALL, ALL), NT)
        if block == 1:
            part = part + dot3(pair(dq2, ALL, ALL), pair(w2.at[0], ALL, ALL), NT)
        grad = part * gain_row
        hat = xhat[rows]
        inner = jnp.mean(grad * hat, axis=1, keepdims=True)
        return rstd[rows] * (grad - jnp.mean(grad, axis=1, keepdims=True) - hat * inner)

    back = [
        remote(dhalo.at[0], halo_in.at[1], dh_send.at[0], dh_recv.at[0], before),
        remote(dhalo.at[1], halo_in.at[0], dh_send.at[1], dh_recv.at[1], after),
    ]
    outs = []

    def write(src, dst, sem):
        copy = pltpu.make_async_copy(src, dst, sem)
        copy.start()
        outs.append(copy)

    def finish(q):
        arrived(7, q)
        lanes = slice(q * LANES, (q + 1) * LANES)
        for i, ref in enumerate((d_q, d_k, d_v)):
            write(full.at[q, pl.ds(i * D, D)], ref.at[:, pl.ds(q * LANES, LANES)], out_sem.at[2 + q * 7 + i])
        for i in range(4):
            write(
                full.at[q, pl.ds(3 * D + i * LANES, LANES)],
                d_o.at[pl.ds(q * LANES, LANES), pl.ds(i * LANES, LANES)],
                out_sem.at[2 + q * 7 + 3 + i],
            )
        dg_acc[...] += (
            full[q, :D] * wf[0, :, lanes] + full[q, D : 2 * D] * wf[1, :, lanes] + full[q, 2 * D : 3 * D] * wf[2, :, lanes]
        )

    dhalo[0] = d_hidden(0)
    step(1, 3)
    step(2, 2)
    step(3, 1)
    step(4, 0)
    dhalo[1] = d_hidden(2)
    step(3, 2)
    step(2, 3)
    step(4, 1)
    step(5, 0)
    dtok_buf[...] = d_hidden(1) + cotf[...]
    step(3, 3)
    step(4, 2)
    step(5, 1)
    step(6, 0)
    res_buf[...] = dot3(pair(o2, ALL, ALL), pair(w2.at[3], ALL, ALL)) + xwin[ROWS : 2 * ROWS]
    write(res_buf, result, out_sem.at[0])
    dg_acc[...] = jnp.zeros_like(dg_acc)
    step(4, 3)
    step(5, 2)
    step(6, 1)
    step(7, 0)
    step(6, 2)
    step(5, 3)
    back[0].start()
    back[1].start()
    step(7, 1)
    step(6, 3)
    finish(0)
    step(7, 2)
    finish(1)
    for copy in back:
        copy.wait_recv()
    dtok_buf[...] = dtok_buf[...] + (halo_in[0] + halo_in[1])
    write(dtok_buf, d_tokens, out_sem.at[1])
    step(7, 3)
    finish(2)
    finish(3)
    d_gain[...] = jnp.sum(dg_acc[...].T, axis=0, keepdims=True) / gain_row
    to_after.wait_send()
    to_before.wait_send()
    for copy in back:
        copy.wait_send()
    for q in range(QUARTERS):
        for level in range(8):
            for copy in copies(level, q):
                copy.wait_send()
    for copy in outs:
        copy.wait()


def layer(nlist, ncount, tokens, gain, wq, wk, wv, wo, cot):
    vmem = pl.BlockSpec(memory_space=pltpu.VMEM)
    smem = pl.BlockSpec(memory_space=pltpu.SMEM)
    hbm = pl.BlockSpec(memory_space=pl.ANY)
    shape = jax.ShapeDtypeStruct
    dma = pltpu.SemaphoreType.DMA
    v = pltpu.VMEM
    wide = HEADS * LANES
    scratch = [
        v((WIN, D), F32),
        v((4, D, D), F32),
        v((ROWS, D), F32),
        v((WIN, D), F32),
        v((WIN, 1), F32),
        v((2, D, WIN), BF16),
        v((4, 2, D, D), BF16),
        v((2, ROWS, D), BF16),
        v((WIN, wide), BF16),
        v((WIN, wide), BF16),
        v((wide, WIN), BF16),
        v((wide, WIN), BF16),
        v((ROWS, 2 * wide), BF16),
        v((ROWS, 2 * wide), BF16),
        v((D, ROWS), F32),
        v((WIN, ROWS), F32),
        v((2, WIN, D), BF16),
        v((2, WIN, D), BF16),
        v((2, ROWS, D), BF16),
        v((2, ROWS, D), BF16),
        v((4, 2048, LANES), F32),
        v((4, 1024, LANES), F32),
        v((4, 2, 3, 128, LANES), F32),
        v((4, 2, 128, LANES), F32),
        v((4, 2, 3, 32, LANES), F32),
        v((4, 64, LANES), F32),
        v((4, 7, 8, LANES), F32),
        v((4, 2048, LANES), F32),
        v((2, ROWS, D), F32),
        v((2, ROWS, D), F32),
        v((ROWS, D), F32),
        v((ROWS, D), F32),
        v((D, LANES), F32),
        dma((6,)),
        dma((2,)),
        dma((2,)),
    ]
    for peers in ((4,), (4, 6), (4, 6), (4, 7), (4, 7), (4, 6), (4, 6), (4,)):
        scratch += [dma(peers), dma(peers)]
    scratch += [dma((2,)), dma((2,)), dma((30,))]
    return pl.pallas_call(
        kernel,
        out_shape=(
            shape((ROWS, D), F32),
            shape((ROWS, D), F32),
            shape((1, D), F32),
            shape((D, D), F32),
            shape((D, D), F32),
            shape((D, D), F32),
            shape((D, D), F32),
        ),
        in_specs=[smem] * 2 + [hbm, vmem] + [hbm] * 5,
        out_specs=(hbm, hbm, vmem, hbm, hbm, hbm, hbm),
        scratch_shapes=scratch,
        compiler_params=pltpu.CompilerParams(
            collective_id=0, has_side_effects=True, vmem_limit_bytes=60 << 20
        ),
        name="patch_layer",
    )(nlist, ncount, tokens, gain, wq, wk, wv, wo, cot)


PARTS = 4


def write_kernel(*refs):
    arrays = (len(refs) - 2) // 3
    load_sem, store_sem = refs[-2:]
    loads, stores = [], []
    for i in range(arrays):
        src, dst, buf = refs[i], refs[arrays + i], refs[2 * arrays + i]
        rows = src.shape[0]
        parts = PARTS if rows >= 8 * PARTS else 1
        for j in range(parts):
            block = pl.ds(j * (rows // parts), rows // parts)
            loads.append(pltpu.make_async_copy(src.at[block], buf.at[block], load_sem.at[i, j]))
            stores.append(pltpu.make_async_copy(buf.at[block], dst.at[block], store_sem.at[i, j]))
    for load in loads:
        load.start()
    for load, store in zip(loads, stores):
        load.wait()
        store.start()
    for store in stores:
        store.wait()


def written(*arrays):
    hbm = pl.BlockSpec(memory_space=pl.ANY)
    sems = pltpu.SemaphoreType.DMA((len(arrays), PARTS))
    return pl.pallas_call(
        write_kernel,
        out_shape=tuple(jax.ShapeDtypeStruct(a.shape, a.dtype) for a in arrays),
        in_specs=[hbm] * len(arrays),
        out_specs=(hbm,) * len(arrays),
        scratch_shapes=[pltpu.VMEM(a.shape, a.dtype) for a in arrays] + [sems, sems],
        compiler_params=pltpu.CompilerParams(vmem_limit_bytes=60 << 20),
        name="write_results",
    )(*arrays)


def body(tokens, gain, wq, wk, wv, wo, nlist, ncount, cot):
    results = layer(nlist, ncount, tokens, gain[None, :], wq, wk, wv, wo, cot)
    result, d_tokens, d_gain, d_q, d_k, d_v, d_o = written(*results)
    return (result, d_tokens, d_gain[0], d_q, d_k, d_v, d_o)


def solution(mesh):
    rows = P(("space", "slab"), None)
    return jax.shard_map(
        body,
        mesh=mesh,
        in_specs=(rows, P(), P(), P(), P(), P(), rows, P(("space", "slab")), rows),
        out_specs=(rows, rows, P(), P(), P(), P(), P()),
        check_vma=False,
    )
```

```python
import jax
import jax.numpy as jnp
from jax import lax
from jax.experimental import pallas as pl
from jax.experimental.pallas import tpu as pltpu
from jax.sharding import PartitionSpec as P

MESH = pl.DeviceIdType.MESH
F32 = jnp.float32
BF16 = jnp.bfloat16
HEADS = 8
PT = 128
D = 512
HD = D // HEADS
ROWS = 256
WIN = 3 * ROWS
NX, NY, NZ = 4, 4, 8
QUARTERS = 4
LANES = 128

NN = (((1,), (0,)), ((), ()))
NT = (((1,), (1,)), ((), ()))


def device(x, y, z, core):
    return {"space": (x * NZ + z) * 2 + core, "slab": y}


def split(value):
    high = value.astype(BF16)
    return high, (value - high.astype(F32)).astype(BF16)


def dot(left, right, dims=NN):
    return lax.dot_general(left, right, dims, preferred_element_type=F32)


def dot3(left, right, dims=NN):
    lh, ll = left
    rh, rl = right
    return dot(lh, rh, dims) + (dot(lh, rl, dims) + dot(ll, rh, dims))


def pair(ref, *index):
    return ref[(0,) + index], ref[(1,) + index]


def put(ref, value, *index):
    high, low = split(value)
    ref[(0,) + index] = high
    ref[(1,) + index] = low
    return high, low


ALL = slice(None)


def at(start, size, step=None):
    return pl.ds(pl.multiple_of(start, step or size), size)


def packed(value):
    high = value.astype(BF16).astype(F32)
    low = value - high
    first = lax.broadcasted_iota(jnp.int32, value.shape, 1) < HD
    high_r, low_r = pltpu.roll(high, HD, 1), pltpu.roll(low, HD, 1)
    hl = (jnp.where(first, high, low_r).astype(BF16), jnp.where(first, high_r, low).astype(BF16))
    lh = (jnp.where(first, low, high_r).astype(BF16), jnp.where(first, low_r, high).astype(BF16))
    return hl, lh


def kernel(
    nlist, ncount, tok, gain, wq, wk, wv, wo, cot,
    result, d_tokens, d_gain, d_q, d_k, d_v, d_o,
    xwin, wf, cotf, xhat, rstd, hid_t, w2, cot2, kp, vp, kt, vt, qp, dop, do_t, bias, dk2, dv2, dq2, o2,
    g, r0, r1, acc2, r2, acc3, r3, full, dhalo, halo_in, res_buf, dtok_buf, dg_acc,
    load_sem, tok_send, tok_recv, level_send, level_recv, dh_send, dh_recv, out_sem,
):
    s = lax.axis_index("space")
    y = lax.axis_index("slab")
    count = NX * NZ * 2
    x, z, c = s // (2 * NZ), (s // 2) % NZ, s % 2
    partner = device(x, y, z, 1 - c)
    other = {"space": (s + count - 1 + 2 * c) % count, "slab": y}
    xs = [(x + d) % NX for d in range(NX)]
    ys = [(y + d) % NY for d in range(NY)]
    zs = [(z + d) % NZ for d in range(NZ)]
    along_x = [device(i, y, z, c) for i in xs]
    along_y = [device(x, i, z, c) for i in ys]
    along_z = [device(x, y, i, c) for i in zs]

    loads = [pltpu.make_async_copy(tok, xwin.at[pl.ds(0, ROWS)], load_sem.at[0])]
    for i, ref in enumerate((wq, wk, wv, wo)):
        loads.append(pltpu.make_async_copy(ref, wf.at[i], load_sem.at[1 + i]))
    loads.append(pltpu.make_async_copy(cot, cotf, load_sem.at[5]))
    for load in loads:
        load.start()

    barrier = pltpu.get_barrier_semaphore()
    everyone = [partner, other] + along_x[1:] + along_y[1:] + along_z[1:]
    for peer in everyone:
        pl.semaphore_signal(barrier, inc=1, device_id=peer, device_id_type=MESH)
    pl.semaphore_wait(barrier, len(everyone))

    def remote(src, dst, send_sem, recv_sem, peer):
        return pltpu.make_async_remote_copy(src, dst, send_sem, recv_sem, device_id=peer, device_id_type=MESH)

    to_far = remote(tok, xwin.at[pl.ds(2 * ROWS, ROWS)], tok_send.at[1], tok_recv.at[1], other)
    to_near = remote(tok, xwin.at[pl.ds(ROWS, ROWS)], tok_send.at[0], tok_recv.at[0], partner)
    to_far.start()
    to_near.start()

    gain_row = gain[...]
    for b in range(6):
        name = (2, 4 * (1 - c), 4 * c)[b // 2] + b % 2
        for p in range(2):
            if b == p:
                flag = 0.0
            else:
                flag = -1e30
                for j in range(3):
                    live = jnp.logical_and(nlist[p, j] == name, j < ncount[p])
                    flag = jnp.where(live, 0.0, flag)
            bias[b * PT : (b + 1) * PT, p * PT : (p + 1) * PT] = jnp.full((PT, PT), flag, F32)

    def keys_values(block):
        rows = slice(block * ROWS, (block + 1) * ROWS)
        tokens = xwin[rows]
        centred = tokens - jnp.mean(tokens, axis=1, keepdims=True)
        inv = lax.rsqrt(jnp.mean(centred * centred, axis=1, keepdims=True) + 1e-5)
        hat = centred * inv
        xhat[rows] = hat
        rstd[rows] = inv
        hidden = hat * gain_row
        put(hid_t, hidden.T, ALL, rows)
        hidden2 = split(hidden)
        for i, pack, turned in ((1, kp, kt), (2, vp, vt)):
            value = dot3(hidden2, pair(w2.at[i], ALL, ALL))
            for hp in range(HEADS // 2):
                hl, _ = packed(value[:, hp * LANES : (hp + 1) * LANES])
                for half in range(2):
                    h = 2 * hp + half
                    pack[rows, h * LANES : (h + 1) * LANES] = hl[half]
            high, low = split(value.T)
            for h in range(HEADS):
                turned[h * LANES : h * LANES + HD, rows] = high[h * HD : (h + 1) * HD]
                turned[h * LANES + HD : (h + 1) * LANES, rows] = low[h * HD : (h + 1) * HD]
        return hidden2

    def pack_rows(pack, value):
        for hp in range(HEADS // 2):
            hl, lh = packed(value[:, hp * LANES : (hp + 1) * LANES])
            for half in range(2):
                h = 2 * hp + half
                pack[:, h * 2 * LANES : h * 2 * LANES + LANES] = hl[half]
                pack[:, h * 2 * LANES + LANES : (h + 1) * 2 * LANES] = lh[half]

    loads[0].wait()
    loads[2].wait()
    put(w2.at[1], wf[1], ALL, ALL)
    loads[3].wait()
    put(w2.at[2], wf[2], ALL, ALL)
    hidden2 = keys_values(0)
    loads[1].wait()
    put(w2.at[0], wf[0], ALL, ALL)
    pack_rows(qp, dot3(hidden2, pair(w2.at[0], ALL, ALL)) * HD**-0.5)
    loads[4].wait()
    put(w2.at[3], wf[3], ALL, ALL)
    loads[5].wait()
    put(cot2, cotf[...], ALL, ALL)
    d_mixed = dot3(pair(cot2, ALL, ALL), pair(w2.at[3], ALL, ALL), NT)
    pack_rows(dop, d_mixed)
    do_t[...] = d_mixed.T
    to_near.wait_recv()
    keys_values(1)
    to_far.wait_recv()
    keys_values(2)

    half_a = c * 1024
    half_b = half_a + 512
    x_rows, y_rows = half_a + x * 128, half_b + y * 128
    xy_rows, yx_rows = x_rows + y * 32, y_rows + x * 32
    upper = z // 4
    tile = xy_rows * (1 - upper) + yx_rows * upper + (z % 4) * 8

    def copies(level, q):
        if level == 0:
            return [(g.at[q, at((1 - c) * 1024, 1024)], r0.at[q], partner)]
        if level == 7:
            return [(full.at[q, at(c * 1024, 1024)], full.at[q, at(c * 1024, 1024)], partner)]
        if level == 3:
            return [(acc3.at[q, at(zs[d] * 8, 8)], r3.at[q, d - 1], along_z[d]) for d in range(1, NZ)]
        if level == 4:
            return [(full.at[q, at(tile, 8)], full.at[q, at(tile, 8)], along_z[d]) for d in range(1, NZ)]
        found = []
        for d in range(1, 4):
            if level == 1:
                found.append((g.at[q, at(half_a + xs[d] * 128, 128)], r1.at[q, 0, d - 1], along_x[d]))
                found.append((g.at[q, at(half_b + ys[d] * 128, 128)], r1.at[q, 1, d - 1], along_y[d]))
            elif level == 2:
                found.append((acc2.at[q, 0, at(ys[d] * 32, 32)], r2.at[q, 0, d - 1], along_y[d]))
                found.append((acc2.at[q, 1, at(xs[d] * 32, 32)], r2.at[q, 1, d - 1], along_x[d]))
            elif level == 5:
                found.append((full.at[q, at(xy_rows, 32)], full.at[q, at(xy_rows, 32)], along_y[d]))
                found.append((full.at[q, at(yx_rows, 32)], full.at[q, at(yx_rows, 32)], along_x[d]))
            else:
                found.append((full.at[q, at(x_rows, 128)], full.at[q, at(x_rows, 128)], along_x[d]))
                found.append((full.at[q, at(y_rows, 128)], full.at[q, at(y_rows, 128)], along_y[d]))
        return found

    def go(level, q):
        for src, dst, peer in copies(level, q):
            remote(src, dst, level_send.at[level, q], level_recv.at[level, q], peer).start()

    def wait_all(level, q, sem):
        whole = (r0, r1, r2, r3)[level].at[q] if level < 4 else full.at[q, pl.ds(0, (56, 192, 768, 1024)[level - 4])]
        pltpu.make_async_copy(whole, whole, sem).wait()

    def arrived(level, q):
        wait_all(level, q, level_recv.at[level, q])

    def left_here(level, q):
        wait_all(level, q, level_send.at[level, q])

    def step(level, q):
        arrived(level - 1, q)
        if level >= 2:
            left_here(level - 2, q)
        if level == 1:
            mine = at(c * 1024, 1024)
            g[q, mine] = g[q, mine] + r0[q]
        elif level == 2:
            for i, rows in enumerate((x_rows, y_rows)):
                acc2[q, i] = (g[q, at(rows, 128)] + r1[q, i, 0]) + (r1[q, i, 1] + r1[q, i, 2])
        elif level == 3:
            for i, row in enumerate((y * 32, x * 32)):
                acc3[q, i * 32 : i * 32 + 32] = (acc2[q, i, at(row, 32)] + r2[q, i, 0]) + (r2[q, i, 1] + r2[q, i, 2])
        elif level == 4:
            total = acc3[q, at(z * 8, 8)]
            for d in range(7):
                total = total + r3[q, d]
            full[q, at(tile, 8)] = total
        go(level, q)

    @pl.loop(0, QUARTERS)
    def _(hp):
        lanes = at(hp * LANES, LANES)
        first = lax.broadcasted_iota(jnp.int32, (WIN, LANES), 1) < HD
        sums_k, sums_v, mixed_ts, dq_ts = [], [], [], []
        heads = []
        for half in range(2):
            h = hp * 2 + half
            double = at(h * 2 * LANES, 2 * LANES)
            k_h, v_h = kp[:, at(h * LANES, LANES)], vp[:, at(h * LANES, LANES)]
            q_h, do_h = qp[:, double], dop[:, double]
            scores = dot(jnp.concatenate([k_h, k_h], axis=1), q_h, NT) + bias[...]
            d_prob = dot(jnp.concatenate([v_h, v_h], axis=1), do_h, NT)
            heads.append((h, q_h[:, :LANES], do_h[:, :LANES], scores, d_prob))
        probs = []
        for h, q_hl, do_hl, scores, d_prob in heads:
            weights = jnp.exp(scores - jnp.max(scores, axis=0, keepdims=True))
            prob = weights * (1.0 / jnp.sum(weights, axis=0, keepdims=True))
            p_high, p_low = split(prob)
            v_t = vt[at(h * LANES, LANES)]
            both = dot(v_t, p_high) + dot(v_t, p_low)
            mixed_t = both[:HD] + both[HD:]
            mixed_ts.append(mixed_t)
            sum_v = dot(p_high, do_hl) + dot(p_low, do_hl)
            sums_v.append(sum_v + pltpu.roll(sum_v, HD, 1))
            probs.append(prob)
        for (h, q_hl, do_hl, scores, d_prob), prob, mixed_t in zip(heads, probs, mixed_ts):
            inner = jnp.sum(mixed_t * do_t[at(h * HD, HD)], axis=0, keepdims=True)
            ds_high, ds_low = split(prob * (d_prob - inner))
            k_t = kt[at(h * LANES, LANES)]
            both = dot(k_t, ds_high) + dot(k_t, ds_low)
            dq_ts.append((both[:HD] + both[HD:]) * HD**-0.5)
            sum_k = dot(ds_high, q_hl) + dot(ds_low, q_hl)
            sums_k.append(sum_k + pltpu.roll(sum_k, HD, 1))
        dk_pair = put(dk2, jnp.where(first, sums_k[0], sums_k[1]), ALL, lanes)
        dv_pair = put(dv2, jnp.where(first, sums_v[0], sums_v[1]), ALL, lanes)
        dq_pair = put(dq2, jnp.concatenate(dq_ts, axis=0).T, ALL, lanes)
        @pl.when(hp >= 1)
        def _():
            step(1, hp - 1)

        mixed_t = jnp.concatenate(mixed_ts, axis=0)
        put(o2, mixed_t.T, ALL, lanes)
        kv = tuple(jnp.concatenate([a, b], axis=1) for a, b in zip(dk_pair, dv_pair))
        grad_kv = dot3(pair(hid_t, ALL, ALL), kv)
        g[hp, :D] = dot3(pair(hid_t, ALL, slice(0, ROWS)), dq_pair)
        g[hp, D : 2 * D] = grad_kv[:, :LANES]
        g[hp, 2 * D : 3 * D] = grad_kv[:, LANES:]
        grad_o = dot3(split(mixed_t), pair(cot2, ALL, ALL))
        for i in range(4):
            g[hp, 3 * D + i * LANES : 3 * D + (i + 1) * LANES] = grad_o[:, i * LANES : (i + 1) * LANES]
        go(0, hp)
        for level in range(2, 4):

            @pl.when(hp >= level)
            def _(level=level):
                step(level, hp - level)

    def d_hidden(block):
        rows = slice(block * ROWS, (block + 1) * ROWS)
        part = dot3(pair(dk2, rows, ALL), pair(w2.at[1], ALL, ALL), NT)
        part = part + dot3(pair(dv2, rows, ALL), pair(w2.at[2], ALL, ALL), NT)
        if block == 0:
            part = part + dot3(pair(dq2, ALL, ALL), pair(w2.at[0], ALL, ALL), NT)
        grad = part * gain_row
        hat = xhat[rows]
        inner = jnp.mean(grad * hat, axis=1, keepdims=True)
        return rstd[rows] * (grad - jnp.mean(grad, axis=1, keepdims=True) - hat * inner)

    back = [
        remote(dhalo.at[0], halo_in.at[0], dh_send.at[0], dh_recv.at[0], partner),
        remote(dhalo.at[1], halo_in.at[1], dh_send.at[1], dh_recv.at[1], other),
    ]
    outs = []

    def write(src, dst, sem):
        copy = pltpu.make_async_copy(src, dst, sem)
        copy.start()
        outs.append(copy)

    def finish(q):
        arrived(7, q)
        lanes = slice(q * LANES, (q + 1) * LANES)
        for i, ref in enumerate((d_q, d_k, d_v)):
            write(full.at[q, pl.ds(i * D, D)], ref.at[:, pl.ds(q * LANES, LANES)], out_sem.at[2 + q * 7 + i])
        for i in range(4):
            write(
                full.at[q, pl.ds(3 * D + i * LANES, LANES)],
                d_o.at[pl.ds(q * LANES, LANES), pl.ds(i * LANES, LANES)],
                out_sem.at[2 + q * 7 + 3 + i],
            )
        dg_acc[...] += (
            full[q, :D] * wf[0, :, lanes] + full[q, D : 2 * D] * wf[1, :, lanes] + full[q, 2 * D : 3 * D] * wf[2, :, lanes]
        )

    dhalo[0] = d_hidden(1)
    step(1, 3)
    step(2, 2)
    step(3, 1)
    step(4, 0)
    dhalo[1] = d_hidden(2)
    step(3, 2)
    step(2, 3)
    step(4, 1)
    step(5, 0)
    dtok_buf[...] = d_hidden(0) + cotf[...]
    step(3, 3)
    step(4, 2)
    step(5, 1)
    step(6, 0)
    res_buf[...] = dot3(pair(o2, ALL, ALL), pair(w2.at[3], ALL, ALL)) + xwin[:ROWS]
    write(res_buf, result, out_sem.at[0])
    dg_acc[...] = jnp.zeros_like(dg_acc)
    step(4, 3)
    step(5, 2)
    step(6, 1)
    step(7, 0)
    step(6, 2)
    step(5, 3)
    back[0].start()
    back[1].start()
    step(7, 1)
    step(6, 3)
    finish(0)
    step(7, 2)
    finish(1)
    for copy in back:
        copy.wait_recv()
    dtok_buf[...] = dtok_buf[...] + (halo_in[0] + halo_in[1])
    write(dtok_buf, d_tokens, out_sem.at[1])
    step(7, 3)
    finish(2)
    finish(3)
    d_gain[...] = jnp.sum(dg_acc[...].T, axis=0, keepdims=True) / gain_row
    to_far.wait_send()
    to_near.wait_send()
    for copy in back:
        copy.wait_send()
    for q in range(QUARTERS):
        left_here(6, q)
        left_here(7, q)
    for copy in outs:
        copy.wait()


def layer(nlist, ncount, tokens, gain, wq, wk, wv, wo, cot):
    vmem = pl.BlockSpec(memory_space=pltpu.VMEM)
    smem = pl.BlockSpec(memory_space=pltpu.SMEM)
    hbm = pl.BlockSpec(memory_space=pl.ANY)
    shape = jax.ShapeDtypeStruct
    dma = pltpu.SemaphoreType.DMA
    v = pltpu.VMEM
    wide = HEADS * LANES
    scratch = [
        v((WIN, D), F32),
        v((4, D, D), F32),
        v((ROWS, D), F32),
        v((WIN, D), F32),
        v((WIN, 1), F32),
        v((2, D, WIN), BF16),
        v((4, 2, D, D), BF16),
        v((2, ROWS, D), BF16),
        v((WIN, wide), BF16),
        v((WIN, wide), BF16),
        v((wide, WIN), BF16),
        v((wide, WIN), BF16),
        v((ROWS, 2 * wide), BF16),
        v((ROWS, 2 * wide), BF16),
        v((D, ROWS), F32),
        v((WIN, ROWS), F32),
        v((2, WIN, D), BF16),
        v((2, WIN, D), BF16),
        v((2, ROWS, D), BF16),
        v((2, ROWS, D), BF16),
        v((4, 2048, LANES), F32),
        v((4, 1024, LANES), F32),
        v((4, 2, 3, 128, LANES), F32),
        v((4, 2, 128, LANES), F32),
        v((4, 2, 3, 32, LANES), F32),
        v((4, 64, LANES), F32),
        v((4, 7, 8, LANES), F32),
        v((4, 2048, LANES), F32),
        v((2, ROWS, D), F32),
        v((2, ROWS, D), F32),
        v((ROWS, D), F32),
        v((ROWS, D), F32),
        v((D, LANES), F32),
        dma((6,)),
        dma((2,)),
        dma((2,)),
    ]
    scratch += [dma((8, QUARTERS)), dma((8, QUARTERS))]
    scratch += [dma((2,)), dma((2,)), dma((30,))]
    return pl.pallas_call(
        kernel,
        out_shape=(
            shape((ROWS, D), F32),
            shape((ROWS, D), F32),
            shape((1, D), F32),
            shape((D, D), F32),
            shape((D, D), F32),
            shape((D, D), F32),
            shape((D, D), F32),
        ),
        in_specs=[smem] * 2 + [hbm, vmem] + [hbm] * 5,
        out_specs=(hbm, hbm, vmem, hbm, hbm, hbm, hbm),
        scratch_shapes=scratch,
        compiler_params=pltpu.CompilerParams(
            collective_id=0, has_side_effects=True, vmem_limit_bytes=60 << 20
        ),
        name="patch_layer",
    )(nlist, ncount, tokens, gain, wq, wk, wv, wo, cot)


PARTS = 4


def write_kernel(*refs):
    arrays = (len(refs) - 2) // 3
    load_sem, store_sem = refs[-2:]
    loads, stores = [], []
    for i in range(arrays):
        src, dst, buf = refs[i], refs[arrays + i], refs[2 * arrays + i]
        rows = src.shape[0]
        parts = PARTS if rows >= 8 * PARTS else 1
        for j in range(parts):
            block = pl.ds(j * (rows // parts), rows // parts)
            loads.append(pltpu.make_async_copy(src.at[block], buf.at[block], load_sem.at[i, j]))
            stores.append(pltpu.make_async_copy(buf.at[block], dst.at[block], store_sem.at[i, j]))
    for load in loads:
        load.start()
    for load, store in zip(loads, stores):
        load.wait()
        store.start()
    for store in stores:
        store.wait()


def written(*arrays):
    hbm = pl.BlockSpec(memory_space=pl.ANY)
    sems = pltpu.SemaphoreType.DMA((len(arrays), PARTS))
    return pl.pallas_call(
        write_kernel,
        out_shape=tuple(jax.ShapeDtypeStruct(a.shape, a.dtype) for a in arrays),
        in_specs=[hbm] * len(arrays),
        out_specs=(hbm,) * len(arrays),
        scratch_shapes=[pltpu.VMEM(a.shape, a.dtype) for a in arrays] + [sems, sems],
        compiler_params=pltpu.CompilerParams(vmem_limit_bytes=60 << 20),
        name="write_results",
    )(*arrays)


def body(tokens, gain, wq, wk, wv, wo, nlist, ncount, cot):
    results = layer(nlist, ncount, tokens, gain[None, :], wq, wk, wv, wo, cot)
    result, d_tokens, d_gain, d_q, d_k, d_v, d_o = written(*results)
    return (result, d_tokens, d_gain[0], d_q, d_k, d_v, d_o)


def solution(mesh):
    rows = P(("space", "slab"), None)
    return jax.shard_map(
        body,
        mesh=mesh,
        in_specs=(rows, P(), P(), P(), P(), P(), rows, P(("space", "slab")), rows),
        out_specs=(rows, rows, P(), P(), P(), P(), P()),
        check_vma=False,
    )
```

```python
import jax
import jax.numpy as jnp
from jax import lax
from jax.experimental import pallas as pl
from jax.experimental.pallas import tpu as pltpu
from jax.sharding import PartitionSpec as P

MESH = pl.DeviceIdType.MESH
F32 = jnp.float32
BF16 = jnp.bfloat16
HEADS = 8
PT = 128
D = 512
HD = D // HEADS
ROWS = 256
WIN = 3 * ROWS
NX, NY, NZ = 4, 4, 8
QUARTERS = 4
LANES = 128

NN = (((1,), (0,)), ((), ()))
NT = (((1,), (1,)), ((), ()))


def device(x, y, z, core):
    return {"space": (x * NZ + z) * 2 + core, "slab": y}


def split(value):
    high = value.astype(BF16)
    return high, (value - high.astype(F32)).astype(BF16)


def dot(left, right, dims=NN):
    return lax.dot_general(left, right, dims, preferred_element_type=F32)


def dot3(left, right, dims=NN):
    lh, ll = left
    rh, rl = right
    return dot(lh, rh, dims) + (dot(lh, rl, dims) + dot(ll, rh, dims))


def pair(ref, *index):
    return ref[(0,) + index], ref[(1,) + index]


def put(ref, value, *index):
    high, low = split(value)
    ref[(0,) + index] = high
    ref[(1,) + index] = low
    return high, low


ALL = slice(None)


def at(start, size, step=None):
    return pl.ds(pl.multiple_of(start, step or size), size)


def packed(value):
    high = value.astype(BF16).astype(F32)
    low = value - high
    first = lax.broadcasted_iota(jnp.int32, value.shape, 1) < HD
    high_r, low_r = pltpu.roll(high, HD, 1), pltpu.roll(low, HD, 1)
    hl = (jnp.where(first, high, low_r).astype(BF16), jnp.where(first, high_r, low).astype(BF16))
    lh = (jnp.where(first, low, high_r).astype(BF16), jnp.where(first, low_r, high).astype(BF16))
    return hl, lh


def kernel(
    nlist, ncount, tok, gain, wq, wk, wv, wo, cot,
    full, res_buf, dtok_buf, d_gain,
    xwin, wf, cotf, xhat, rstd, hid_t, w2, cot2, kp, vp, kt, vt, qp, dop, do_t, bias, dk2, dv2, dq2, o2,
    g, r0, r1, acc2, r2, acc3, r3, dhalo, halo_in, dg_acc,
    load_sem, tok_send, tok_recv, level_send, level_recv, dh_send, dh_recv,
):
    s = lax.axis_index("space")
    y = lax.axis_index("slab")
    count = NX * NZ * 2
    x, z, c = s // (2 * NZ), (s // 2) % NZ, s % 2
    partner = device(x, y, z, 1 - c)
    other = {"space": (s + count - 1 + 2 * c) % count, "slab": y}
    xs = [(x + d) % NX for d in range(NX)]
    ys = [(y + d) % NY for d in range(NY)]
    zs = [(z + d) % NZ for d in range(NZ)]
    along_x = [device(i, y, z, c) for i in xs]
    along_y = [device(x, i, z, c) for i in ys]
    along_z = [device(x, y, i, c) for i in zs]

    loads = [pltpu.make_async_copy(tok, xwin.at[pl.ds(0, ROWS)], load_sem.at[0])]
    for i, ref in enumerate((wq, wk, wv, wo)):
        loads.append(pltpu.make_async_copy(ref, wf.at[i], load_sem.at[1 + i]))
    loads.append(pltpu.make_async_copy(cot, cotf, load_sem.at[5]))
    for load in loads:
        load.start()

    barrier = pltpu.get_barrier_semaphore()
    everyone = [partner, other] + along_x[1:] + along_y[1:] + along_z[1:]
    for peer in everyone:
        pl.semaphore_signal(barrier, inc=1, device_id=peer, device_id_type=MESH)
    pl.semaphore_wait(barrier, len(everyone))

    def remote(src, dst, send_sem, recv_sem, peer):
        return pltpu.make_async_remote_copy(src, dst, send_sem, recv_sem, device_id=peer, device_id_type=MESH)

    to_far = remote(tok, xwin.at[pl.ds(2 * ROWS, ROWS)], tok_send.at[1], tok_recv.at[1], other)
    to_near = remote(tok, xwin.at[pl.ds(ROWS, ROWS)], tok_send.at[0], tok_recv.at[0], partner)
    to_far.start()
    to_near.start()

    gain_row = gain[...]
    for b in range(6):
        name = (2, 4 * (1 - c), 4 * c)[b // 2] + b % 2
        for p in range(2):
            if b == p:
                flag = 0.0
            else:
                flag = -1e30
                for j in range(3):
                    live = jnp.logical_and(nlist[p, j] == name, j < ncount[p])
                    flag = jnp.where(live, 0.0, flag)
            bias[b * PT : (b + 1) * PT, p * PT : (p + 1) * PT] = jnp.full((PT, PT), flag, F32)

    def keys_values(block):
        rows = slice(block * ROWS, (block + 1) * ROWS)
        tokens = xwin[rows]
        centred = tokens - jnp.mean(tokens, axis=1, keepdims=True)
        inv = lax.rsqrt(jnp.mean(centred * centred, axis=1, keepdims=True) + 1e-5)
        hat = centred * inv
        xhat[rows] = hat
        rstd[rows] = inv
        hidden = hat * gain_row
        put(hid_t, hidden.T, ALL, rows)
        hidden2 = split(hidden)
        for i, pack, turned in ((1, kp, kt), (2, vp, vt)):
            value = dot3(hidden2, pair(w2.at[i], ALL, ALL))
            for hp in range(HEADS // 2):
                hl, _ = packed(value[:, hp * LANES : (hp + 1) * LANES])
                for half in range(2):
                    h = 2 * hp + half
                    pack[rows, h * LANES : (h + 1) * LANES] = hl[half]
            high, low = split(value.T)
            for h in range(HEADS):
                turned[h * LANES : h * LANES + HD, rows] = high[h * HD : (h + 1) * HD]
                turned[h * LANES + HD : (h + 1) * LANES, rows] = low[h * HD : (h + 1) * HD]
        return hidden2

    def pack_rows(pack, value):
        for hp in range(HEADS // 2):
            hl, lh = packed(value[:, hp * LANES : (hp + 1) * LANES])
            for half in range(2):
                h = 2 * hp + half
                pack[:, h * 2 * LANES : h * 2 * LANES + LANES] = hl[half]
                pack[:, h * 2 * LANES + LANES : (h + 1) * 2 * LANES] = lh[half]

    loads[0].wait()
    loads[2].wait()
    put(w2.at[1], wf[1], ALL, ALL)
    loads[3].wait()
    put(w2.at[2], wf[2], ALL, ALL)
    hidden2 = keys_values(0)
    loads[1].wait()
    put(w2.at[0], wf[0], ALL, ALL)
    pack_rows(qp, dot3(hidden2, pair(w2.at[0], ALL, ALL)) * HD**-0.5)
    loads[4].wait()
    put(w2.at[3], wf[3], ALL, ALL)
    loads[5].wait()
    put(cot2, cotf[...], ALL, ALL)
    d_mixed = dot3(pair(cot2, ALL, ALL), pair(w2.at[3], ALL, ALL), NT)
    pack_rows(dop, d_mixed)
    do_t[...] = d_mixed.T
    to_near.wait_recv()
    keys_values(1)
    to_far.wait_recv()
    keys_values(2)

    half_a = c * 1024
    half_b = half_a + 512
    x_rows, y_rows = half_a + x * 128, half_b + y * 128
    xy_rows, yx_rows = x_rows + y * 32, y_rows + x * 32
    upper = z // 4
    tile = xy_rows * (1 - upper) + yx_rows * upper + (z % 4) * 8

    def copies(level, q):
        if level == 0:
            return [(g.at[q, at((1 - c) * 1024, 1024)], r0.at[q], partner)]
        if level == 7:
            return [(full.at[q, at(c * 1024, 1024)], full.at[q, at(c * 1024, 1024)], partner)]
        if level == 3:
            return [(acc3.at[q, at(zs[d] * 8, 8)], r3.at[q, d - 1], along_z[d]) for d in range(1, NZ)]
        if level == 4:
            return [(full.at[q, at(tile, 8)], full.at[q, at(tile, 8)], along_z[d]) for d in range(1, NZ)]
        found = []
        for d in range(1, 4):
            if level == 1:
                found.append((g.at[q, at(half_a + xs[d] * 128, 128)], r1.at[q, 0, d - 1], along_x[d]))
                found.append((g.at[q, at(half_b + ys[d] * 128, 128)], r1.at[q, 1, d - 1], along_y[d]))
            elif level == 2:
                found.append((acc2.at[q, 0, at(ys[d] * 32, 32)], r2.at[q, 0, d - 1], along_y[d]))
                found.append((acc2.at[q, 1, at(xs[d] * 32, 32)], r2.at[q, 1, d - 1], along_x[d]))
            elif level == 5:
                found.append((full.at[q, at(xy_rows, 32)], full.at[q, at(xy_rows, 32)], along_y[d]))
                found.append((full.at[q, at(yx_rows, 32)], full.at[q, at(yx_rows, 32)], along_x[d]))
            else:
                found.append((full.at[q, at(x_rows, 128)], full.at[q, at(x_rows, 128)], along_x[d]))
                found.append((full.at[q, at(y_rows, 128)], full.at[q, at(y_rows, 128)], along_y[d]))
        return found

    def go(level, q):
        for src, dst, peer in copies(level, q):
            remote(src, dst, level_send.at[level, q], level_recv.at[level, q], peer).start()

    def wait_all(level, q, sem):
        whole = (r0, r1, r2, r3)[level].at[q] if level < 4 else full.at[q, pl.ds(0, (56, 192, 768, 1024)[level - 4])]
        pltpu.make_async_copy(whole, whole, sem).wait()

    def arrived(level, q):
        wait_all(level, q, level_recv.at[level, q])

    def left_here(level, q):
        wait_all(level, q, level_send.at[level, q])

    def step(level, q):
        arrived(level - 1, q)
        if level >= 2:
            left_here(level - 2, q)
        if level == 1:
            mine = at(c * 1024, 1024)
            g[q, mine] = g[q, mine] + r0[q]
        elif level == 2:
            for i, rows in enumerate((x_rows, y_rows)):
                acc2[q, i] = (g[q, at(rows, 128)] + r1[q, i, 0]) + (r1[q, i, 1] + r1[q, i, 2])
        elif level == 3:
            for i, row in enumerate((y * 32, x * 32)):
                acc3[q, i * 32 : i * 32 + 32] = (acc2[q, i, at(row, 32)] + r2[q, i, 0]) + (r2[q, i, 1] + r2[q, i, 2])
        elif level == 4:
            total = acc3[q, at(z * 8, 8)]
            for d in range(7):
                total = total + r3[q, d]
            full[q, at(tile, 8)] = total
        go(level, q)

    @pl.loop(0, QUARTERS)
    def _(hp):
        lanes = at(hp * LANES, LANES)
        first = lax.broadcasted_iota(jnp.int32, (WIN, LANES), 1) < HD
        sums_k, sums_v, mixed_ts, dq_ts = [], [], [], []
        heads = []
        for half in range(2):
            h = hp * 2 + half
            double = at(h * 2 * LANES, 2 * LANES)
            k_h, v_h = kp[:, at(h * LANES, LANES)], vp[:, at(h * LANES, LANES)]
            q_h, do_h = qp[:, double], dop[:, double]
            scores = dot(jnp.concatenate([k_h, k_h], axis=1), q_h, NT) + bias[...]
            d_prob = dot(jnp.concatenate([v_h, v_h], axis=1), do_h, NT)
            heads.append((h, q_h[:, :LANES], do_h[:, :LANES], scores, d_prob))
        probs = []
        for h, q_hl, do_hl, scores, d_prob in heads:
            weights = jnp.exp(scores - jnp.max(scores, axis=0, keepdims=True))
            prob = weights * (1.0 / jnp.sum(weights, axis=0, keepdims=True))
            p_high, p_low = split(prob)
            v_t = vt[at(h * LANES, LANES)]
            both = dot(v_t, p_high) + dot(v_t, p_low)
            mixed_t = both[:HD] + both[HD:]
            mixed_ts.append(mixed_t)
            sum_v = dot(p_high, do_hl) + dot(p_low, do_hl)
            sums_v.append(sum_v + pltpu.roll(sum_v, HD, 1))
            probs.append(prob)
        for (h, q_hl, do_hl, scores, d_prob), prob, mixed_t in zip(heads, probs, mixed_ts):
            inner = jnp.sum(mixed_t * do_t[at(h * HD, HD)], axis=0, keepdims=True)
            ds_high, ds_low = split(prob * (d_prob - inner))
            k_t = kt[at(h * LANES, LANES)]
            both = dot(k_t, ds_high) + dot(k_t, ds_low)
            dq_ts.append((both[:HD] + both[HD:]) * HD**-0.5)
            sum_k = dot(ds_high, q_hl) + dot(ds_low, q_hl)
            sums_k.append(sum_k + pltpu.roll(sum_k, HD, 1))
        dk_pair = put(dk2, jnp.where(first, sums_k[0], sums_k[1]), ALL, lanes)
        dv_pair = put(dv2, jnp.where(first, sums_v[0], sums_v[1]), ALL, lanes)
        dq_pair = put(dq2, jnp.concatenate(dq_ts, axis=0).T, ALL, lanes)
        @pl.when(hp >= 1)
        def _():
            step(1, hp - 1)

        mixed_t = jnp.concatenate(mixed_ts, axis=0)
        put(o2, mixed_t.T, ALL, lanes)
        kv = tuple(jnp.concatenate([a, b], axis=1) for a, b in zip(dk_pair, dv_pair))
        grad_kv = dot3(pair(hid_t, ALL, ALL), kv)
        g[hp, :D] = dot3(pair(hid_t, ALL, slice(0, ROWS)), dq_pair)
        g[hp, D : 2 * D] = grad_kv[:, :LANES]
        g[hp, 2 * D : 3 * D] = grad_kv[:, LANES:]
        grad_o = dot3(split(mixed_t), pair(cot2, ALL, ALL))
        for i in range(4):
            g[hp, 3 * D + i * LANES : 3 * D + (i + 1) * LANES] = grad_o[:, i * LANES : (i + 1) * LANES]
        go(0, hp)
        for level in range(2, 4):

            @pl.when(hp >= level)
            def _(level=level):
                step(level, hp - level)

    def d_hidden(block):
        rows = slice(block * ROWS, (block + 1) * ROWS)
        part = dot3(pair(dk2, rows, ALL), pair(w2.at[1], ALL, ALL), NT)
        part = part + dot3(pair(dv2, rows, ALL), pair(w2.at[2], ALL, ALL), NT)
        if block == 0:
            part = part + dot3(pair(dq2, ALL, ALL), pair(w2.at[0], ALL, ALL), NT)
        grad = part * gain_row
        hat = xhat[rows]
        inner = jnp.mean(grad * hat, axis=1, keepdims=True)
        return rstd[rows] * (grad - jnp.mean(grad, axis=1, keepdims=True) - hat * inner)

    back = [
        remote(dhalo.at[0], halo_in.at[0], dh_send.at[0], dh_recv.at[0], partner),
        remote(dhalo.at[1], halo_in.at[1], dh_send.at[1], dh_recv.at[1], other),
    ]
    def finish(q):
        arrived(7, q)
        lanes = slice(q * LANES, (q + 1) * LANES)
        dg_acc[...] += (
            full[q, :D] * wf[0, :, lanes] + full[q, D : 2 * D] * wf[1, :, lanes] + full[q, 2 * D : 3 * D] * wf[2, :, lanes]
        )

    dhalo[0] = d_hidden(1)
    step(1, 3)
    step(2, 2)
    step(3, 1)
    step(4, 0)
    dhalo[1] = d_hidden(2)
    step(3, 2)
    step(2, 3)
    step(4, 1)
    step(5, 0)
    dtok_buf[...] = d_hidden(0) + cotf[...]
    step(3, 3)
    step(4, 2)
    step(5, 1)
    step(6, 0)
    res_buf[...] = dot3(pair(o2, ALL, ALL), pair(w2.at[3], ALL, ALL)) + xwin[:ROWS]
    dg_acc[...] = jnp.zeros_like(dg_acc)
    step(4, 3)
    step(5, 2)
    step(6, 1)
    step(7, 0)
    step(6, 2)
    step(5, 3)
    back[0].start()
    back[1].start()
    step(7, 1)
    step(6, 3)
    finish(0)
    step(7, 2)
    finish(1)
    for copy in back:
        copy.wait_recv()
    dtok_buf[...] = dtok_buf[...] + (halo_in[0] + halo_in[1])
    step(7, 3)
    finish(2)
    finish(3)
    d_gain[...] = jnp.sum(dg_acc[...].T, axis=0, keepdims=True) / gain_row
    to_far.wait_send()
    to_near.wait_send()
    for copy in back:
        copy.wait_send()
    for q in range(QUARTERS):
        left_here(6, q)
        left_here(7, q)


def layer(nlist, ncount, tokens, gain, wq, wk, wv, wo, cot):
    vmem = pl.BlockSpec(memory_space=pltpu.VMEM)
    smem = pl.BlockSpec(memory_space=pltpu.SMEM)
    hbm = pl.BlockSpec(memory_space=pl.ANY)
    shape = jax.ShapeDtypeStruct
    dma = pltpu.SemaphoreType.DMA
    v = pltpu.VMEM
    wide = HEADS * LANES
    scratch = [
        v((WIN, D), F32),
        v((4, D, D), F32),
        v((ROWS, D), F32),
        v((WIN, D), F32),
        v((WIN, 1), F32),
        v((2, D, WIN), BF16),
        v((4, 2, D, D), BF16),
        v((2, ROWS, D), BF16),
        v((WIN, wide), BF16),
        v((WIN, wide), BF16),
        v((wide, WIN), BF16),
        v((wide, WIN), BF16),
        v((ROWS, 2 * wide), BF16),
        v((ROWS, 2 * wide), BF16),
        v((D, ROWS), F32),
        v((WIN, ROWS), F32),
        v((2, WIN, D), BF16),
        v((2, WIN, D), BF16),
        v((2, ROWS, D), BF16),
        v((2, ROWS, D), BF16),
        v((4, 2048, LANES), F32),
        v((4, 1024, LANES), F32),
        v((4, 2, 3, 128, LANES), F32),
        v((4, 2, 128, LANES), F32),
        v((4, 2, 3, 32, LANES), F32),
        v((4, 64, LANES), F32),
        v((4, 7, 8, LANES), F32),
        v((2, ROWS, D), F32),
        v((2, ROWS, D), F32),
        v((D, LANES), F32),
        dma((6,)),
        dma((2,)),
        dma((2,)),
    ]
    scratch += [dma((8, QUARTERS)), dma((8, QUARTERS))]
    scratch += [dma((2,)), dma((2,))]
    return pl.pallas_call(
        kernel,
        out_shape=(v((QUARTERS, 2048, LANES), F32), v((ROWS, D), F32), v((ROWS, D), F32), v((1, D), F32)),
        in_specs=[smem] * 2 + [hbm, vmem] + [hbm] * 5,
        out_specs=(vmem,) * 4,
        scratch_shapes=scratch,
        compiler_params=pltpu.CompilerParams(
            collective_id=0, has_side_effects=True, vmem_limit_bytes=52 << 20
        ),
        name="patch_layer",
    )(nlist, ncount, tokens, gain, wq, wk, wv, wo, cot)


def write_kernel(full, res, dtok, gain, result, d_tokens, d_gain, d_q, d_k, d_v, d_o, sem):
    pairs = [(res, result), (dtok, d_tokens), (gain, d_gain)]
    for q in range(QUARTERS):
        lanes = pl.ds(q * LANES, LANES)
        for i, ref in enumerate((d_q, d_k, d_v)):
            pairs.append((full.at[q, pl.ds(i * D, D)], ref.at[:, lanes]))
        for i in range(4):
            pairs.append((full.at[q, pl.ds(3 * D + i * LANES, LANES)], d_o.at[lanes, pl.ds(i * LANES, LANES)]))
    copies = [pltpu.make_async_copy(src, dst, sem.at[i]) for i, (src, dst) in enumerate(pairs)]
    for copy in copies:
        copy.start()
    for copy in copies:
        copy.wait()


def written(full, res, dtok, gain):
    shape = jax.ShapeDtypeStruct
    hbm = pl.BlockSpec(memory_space=pl.ANY)
    vmem = pl.BlockSpec(memory_space=pltpu.VMEM)
    rows, row, square = shape((ROWS, D), F32), shape((1, D), F32), shape((D, D), F32)
    held = [pltpu.with_memory_space_constraint(a, pltpu.VMEM) for a in (full, res, dtok, gain)]
    return pl.pallas_call(
        write_kernel,
        out_shape=(rows, rows, row, square, square, square, square),
        in_specs=[vmem] * 4,
        out_specs=(hbm,) * 7,
        scratch_shapes=[pltpu.SemaphoreType.DMA((3 + 7 * QUARTERS,))],
        compiler_params=pltpu.CompilerParams(vmem_limit_bytes=8 << 20),
        name="write_results",
    )(*held)


def body(tokens, gain, wq, wk, wv, wo, nlist, ncount, cot):
    results = layer(nlist, ncount, tokens, gain[None, :], wq, wk, wv, wo, cot)
    result, d_tokens, d_gain, d_q, d_k, d_v, d_o = written(*results)
    return (result, d_tokens, d_gain[0], d_q, d_k, d_v, d_o)


def solution(mesh):
    rows = P(("space", "slab"), None)
    return jax.shard_map(
        body,
        mesh=mesh,
        in_specs=(rows, P(), P(), P(), P(), P(), rows, P(("space", "slab")), rows),
        out_specs=(rows, rows, P(), P(), P(), P(), P()),
        check_vma=False,
    )
```

```python
import jax
import jax.numpy as jnp
from jax import lax
from jax.experimental import pallas as pl
from jax.experimental.pallas import tpu as pltpu
from jax.sharding import PartitionSpec as P

MESH = pl.DeviceIdType.MESH
F32 = jnp.float32
BF16 = jnp.bfloat16
HEADS = 8
PT = 128
D = 512
HD = D // HEADS
ROWS = 256
WIN = 3 * ROWS
NX, NY, NZ = 4, 4, 8
QUARTERS = 4
LANES = 128
FAR = (2, 1, 3)
FAR_Z = (4, 3, 5, 2, 6, 1, 7)

NN = (((1,), (0,)), ((), ()))
NT = (((1,), (1,)), ((), ()))


def device(x, y, z, core):
    return {"space": (x * NZ + z) * 2 + core, "slab": y}


def split(value):
    high = value.astype(BF16)
    return high, (value - high.astype(F32)).astype(BF16)


def dot(left, right, dims=NN):
    return lax.dot_general(left, right, dims, preferred_element_type=F32)


def dot3(left, right, dims=NN):
    lh, ll = left
    rh, rl = right
    return dot(lh, rh, dims) + (dot(lh, rl, dims) + dot(ll, rh, dims))


def pair(ref, *index):
    return ref[(0,) + index], ref[(1,) + index]


def put(ref, value, *index):
    high, low = split(value)
    ref[(0,) + index] = high
    ref[(1,) + index] = low
    return high, low


ALL = slice(None)


def at(start, size, step=None):
    return pl.ds(pl.multiple_of(start, step or size), size)


def packed(value):
    high = value.astype(BF16).astype(F32)
    low = value - high
    first = lax.broadcasted_iota(jnp.int32, value.shape, 1) < HD
    high_r, low_r = pltpu.roll(high, HD, 1), pltpu.roll(low, HD, 1)
    hl = (jnp.where(first, high, low_r).astype(BF16), jnp.where(first, high_r, low).astype(BF16))
    lh = (jnp.where(first, low, high_r).astype(BF16), jnp.where(first, low_r, high).astype(BF16))
    return hl, lh


def kernel(
    nlist, ncount, tok, gain, wq, wk, wv, wo, cot,
    full, res_buf, dtok_buf, d_gain,
    xwin, wf, cotf, xhat, rstd, hid_t, w2, cot2, kp, vp, kt, vt, qp, dop, do_t, bias, dk2, dv2, dq2, o2,
    g, r0, r1, acc2, r2, acc3, r3, dhalo, halo_in, dg_acc,
    load_sem, tok_send, tok_recv, level_send, level_recv, dh_send, dh_recv,
):
    s = lax.axis_index("space")
    y = lax.axis_index("slab")
    count = NX * NZ * 2
    x, z, c = s // (2 * NZ), (s // 2) % NZ, s % 2
    partner = device(x, y, z, 1 - c)
    other = {"space": (s + count - 1 + 2 * c) % count, "slab": y}
    xs = [(x + d) % NX for d in range(NX)]
    ys = [(y + d) % NY for d in range(NY)]
    zs = [(z + d) % NZ for d in range(NZ)]
    along_x = [device(i, y, z, c) for i in xs]
    along_y = [device(x, i, z, c) for i in ys]
    along_z = [device(x, y, i, c) for i in zs]

    loads = [pltpu.make_async_copy(tok, xwin.at[pl.ds(0, ROWS)], load_sem.at[0])]
    for i, ref in enumerate((wq, wk, wv, wo)):
        loads.append(pltpu.make_async_copy(ref, wf.at[i], load_sem.at[1 + i]))
    loads.append(pltpu.make_async_copy(cot, cotf, load_sem.at[5]))
    for load in loads:
        load.start()

    barrier = pltpu.get_barrier_semaphore()
    everyone = [along_z[d] for d in FAR_Z] + [along_x[d] for d in FAR] + [along_y[d] for d in FAR] + [other, partner]
    for peer in everyone:
        pl.semaphore_signal(barrier, inc=1, device_id=peer, device_id_type=MESH)
    pl.semaphore_wait(barrier, len(everyone))

    def remote(src, dst, send_sem, recv_sem, peer):
        return pltpu.make_async_remote_copy(src, dst, send_sem, recv_sem, device_id=peer, device_id_type=MESH)

    to_far = remote(tok, xwin.at[pl.ds(2 * ROWS, ROWS)], tok_send.at[1], tok_recv.at[1], other)
    to_near = remote(tok, xwin.at[pl.ds(ROWS, ROWS)], tok_send.at[0], tok_recv.at[0], partner)
    to_far.start()
    to_near.start()

    gain_row = gain[...]
    for b in range(6):
        name = (2, 4 * (1 - c), 4 * c)[b // 2] + b % 2
        for p in range(2):
            if b == p:
                flag = 0.0
            else:
                flag = -1e30
                for j in range(3):
                    live = jnp.logical_and(nlist[p, j] == name, j < ncount[p])
                    flag = jnp.where(live, 0.0, flag)
            bias[b * PT : (b + 1) * PT, p * PT : (p + 1) * PT] = jnp.full((PT, PT), flag, F32)

    def keys_values(block):
        rows = slice(block * ROWS, (block + 1) * ROWS)
        tokens = xwin[rows]
        centred = tokens - jnp.mean(tokens, axis=1, keepdims=True)
        inv = lax.rsqrt(jnp.mean(centred * centred, axis=1, keepdims=True) + 1e-5)
        hat = centred * inv
        xhat[rows] = hat
        rstd[rows] = inv
        hidden = hat * gain_row
        put(hid_t, hidden.T, ALL, rows)
        hidden2 = split(hidden)
        for i, pack, turned in ((1, kp, kt), (2, vp, vt)):
            value = dot3(hidden2, pair(w2.at[i], ALL, ALL))
            for hp in range(HEADS // 2):
                hl, _ = packed(value[:, hp * LANES : (hp + 1) * LANES])
                for half in range(2):
                    h = 2 * hp + half
                    pack[rows, h * LANES : (h + 1) * LANES] = hl[half]
            high, low = split(value.T)
            for h in range(HEADS):
                turned[h * LANES : h * LANES + HD, rows] = high[h * HD : (h + 1) * HD]
                turned[h * LANES + HD : (h + 1) * LANES, rows] = low[h * HD : (h + 1) * HD]
        return hidden2

    def pack_rows(pack, value):
        for hp in range(HEADS // 2):
            hl, lh = packed(value[:, hp * LANES : (hp + 1) * LANES])
            for half in range(2):
                h = 2 * hp + half
                pack[:, h * 2 * LANES : h * 2 * LANES + LANES] = hl[half]
                pack[:, h * 2 * LANES + LANES : (h + 1) * 2 * LANES] = lh[half]

    loads[0].wait()
    loads[2].wait()
    put(w2.at[1], wf[1], ALL, ALL)
    loads[3].wait()
    put(w2.at[2], wf[2], ALL, ALL)
    hidden2 = keys_values(0)
    loads[1].wait()
    put(w2.at[0], wf[0], ALL, ALL)
    pack_rows(qp, dot3(hidden2, pair(w2.at[0], ALL, ALL)) * HD**-0.5)
    loads[4].wait()
    put(w2.at[3], wf[3], ALL, ALL)
    loads[5].wait()
    put(cot2, cotf[...], ALL, ALL)
    d_mixed = dot3(pair(cot2, ALL, ALL), pair(w2.at[3], ALL, ALL), NT)
    pack_rows(dop, d_mixed)
    do_t[...] = d_mixed.T
    to_near.wait_recv()
    keys_values(1)
    to_far.wait_recv()
    keys_values(2)

    half_a = c * 1024
    half_b = half_a + 512
    x_rows, y_rows = half_a + x * 128, half_b + y * 128
    xy_rows, yx_rows = x_rows + y * 32, y_rows + x * 32
    upper = z // 4
    tile = xy_rows * (1 - upper) + yx_rows * upper + (z % 4) * 8

    def copies(level, q):
        if level == 0:
            return [(g.at[q, at((1 - c) * 1024, 1024)], r0.at[q], partner)]
        if level == 7:
            return [(full.at[q, at(c * 1024, 1024)], full.at[q, at(c * 1024, 1024)], partner)]
        if level == 3:
            return [(acc3.at[q, at(zs[d] * 8, 8)], r3.at[q, d - 1], along_z[d]) for d in FAR_Z]
        if level == 4:
            return [(full.at[q, at(tile, 8)], full.at[q, at(tile, 8)], along_z[d]) for d in FAR_Z]
        found = []
        for d in range(1, 4):
            if level == 1:
                found.append((g.at[q, at(half_a + xs[d] * 128, 128)], r1.at[q, 0, d - 1], along_x[d]))
                found.append((g.at[q, at(half_b + ys[d] * 128, 128)], r1.at[q, 1, d - 1], along_y[d]))
            elif level == 2:
                found.append((acc2.at[q, 0, at(ys[d] * 32, 32)], r2.at[q, 0, d - 1], along_y[d]))
                found.append((acc2.at[q, 1, at(xs[d] * 32, 32)], r2.at[q, 1, d - 1], along_x[d]))
            elif level == 5:
                found.append((full.at[q, at(xy_rows, 32)], full.at[q, at(xy_rows, 32)], along_y[d]))
                found.append((full.at[q, at(yx_rows, 32)], full.at[q, at(yx_rows, 32)], along_x[d]))
            else:
                found.append((full.at[q, at(x_rows, 128)], full.at[q, at(x_rows, 128)], along_x[d]))
                found.append((full.at[q, at(y_rows, 128)], full.at[q, at(y_rows, 128)], along_y[d]))
        return found

    def go(level, q):
        for src, dst, peer in copies(level, q):
            remote(src, dst, level_send.at[level, q], level_recv.at[level, q], peer).start()

    def wait_all(level, q, sem):
        whole = (r0, r1, r2, r3)[level].at[q] if level < 4 else full.at[q, pl.ds(0, (56, 192, 768, 1024)[level - 4])]
        pltpu.make_async_copy(whole, whole, sem).wait()

    def arrived(level, q):
        wait_all(level, q, level_recv.at[level, q])

    def left_here(level, q):
        wait_all(level, q, level_send.at[level, q])

    def step(level, q):
        arrived(level - 1, q)
        if level >= 2:
            left_here(level - 2, q)
        if level == 1:
            mine = at(c * 1024, 1024)
            g[q, mine] = g[q, mine] + r0[q]
        elif level == 2:
            for i, rows in enumerate((x_rows, y_rows)):
                acc2[q, i] = (g[q, at(rows, 128)] + r1[q, i, 0]) + (r1[q, i, 1] + r1[q, i, 2])
        elif level == 3:
            for i, row in enumerate((y * 32, x * 32)):
                acc3[q, i * 32 : i * 32 + 32] = (acc2[q, i, at(row, 32)] + r2[q, i, 0]) + (r2[q, i, 1] + r2[q, i, 2])
        elif level == 4:
            total = acc3[q, at(z * 8, 8)]
            for d in range(7):
                total = total + r3[q, d]
            full[q, at(tile, 8)] = total
        go(level, q)

    @pl.loop(0, QUARTERS)
    def _(hp):
        lanes = at(hp * LANES, LANES)
        first = lax.broadcasted_iota(jnp.int32, (WIN, LANES), 1) < HD
        sums_k, sums_v, mixed_ts, dq_ts = [], [], [], []
        heads = []
        for half in range(2):
            h = hp * 2 + half
            double = at(h * 2 * LANES, 2 * LANES)
            k_h, v_h = kp[:, at(h * LANES, LANES)], vp[:, at(h * LANES, LANES)]
            q_h, do_h = qp[:, double], dop[:, double]
            scores = dot(jnp.concatenate([k_h, k_h], axis=1), q_h, NT) + bias[...]
            d_prob = dot(jnp.concatenate([v_h, v_h], axis=1), do_h, NT)
            heads.append((h, q_h[:, :LANES], do_h[:, :LANES], scores, d_prob))
        probs = []
        for h, q_hl, do_hl, scores, d_prob in heads:
            weights = jnp.exp(scores - jnp.max(scores, axis=0, keepdims=True))
            prob = weights * (1.0 / jnp.sum(weights, axis=0, keepdims=True))
            p_high, p_low = split(prob)
            v_t = vt[at(h * LANES, LANES)]
            both = dot(v_t, p_high) + dot(v_t, p_low)
            mixed_t = both[:HD] + both[HD:]
            mixed_ts.append(mixed_t)
            sum_v = dot(p_high, do_hl) + dot(p_low, do_hl)
            sums_v.append(sum_v + pltpu.roll(sum_v, HD, 1))
            probs.append(prob)
        for (h, q_hl, do_hl, scores, d_prob), prob, mixed_t in zip(heads, probs, mixed_ts):
            inner = jnp.sum(mixed_t * do_t[at(h * HD, HD)], axis=0, keepdims=True)
            ds_high, ds_low = split(prob * (d_prob - inner))
            k_t = kt[at(h * LANES, LANES)]
            both = dot(k_t, ds_high) + dot(k_t, ds_low)
            dq_ts.append((both[:HD] + both[HD:]) * HD**-0.5)
            sum_k = dot(ds_high, q_hl) + dot(ds_low, q_hl)
            sums_k.append(sum_k + pltpu.roll(sum_k, HD, 1))
        dk_pair = put(dk2, jnp.where(first, sums_k[0], sums_k[1]), ALL, lanes)
        dv_pair = put(dv2, jnp.where(first, sums_v[0], sums_v[1]), ALL, lanes)
        dq_pair = put(dq2, jnp.concatenate(dq_ts, axis=0).T, ALL, lanes)
        @pl.when(hp >= 1)
        def _():
            step(1, hp - 1)

        mixed_t = jnp.concatenate(mixed_ts, axis=0)
        put(o2, mixed_t.T, ALL, lanes)
        kv = tuple(jnp.concatenate([a, b], axis=1) for a, b in zip(dk_pair, dv_pair))
        grad_kv = dot3(pair(hid_t, ALL, ALL), kv)
        g[hp, :D] = dot3(pair(hid_t, ALL, slice(0, ROWS)), dq_pair)
        g[hp, D : 2 * D] = grad_kv[:, :LANES]
        g[hp, 2 * D : 3 * D] = grad_kv[:, LANES:]
        grad_o = dot3(split(mixed_t), pair(cot2, ALL, ALL))
        for i in range(4):
            g[hp, 3 * D + i * LANES : 3 * D + (i + 1) * LANES] = grad_o[:, i * LANES : (i + 1) * LANES]
        go(0, hp)
        for level in range(2, 4):

            @pl.when(hp >= level)
            def _(level=level):
                step(level, hp - level)

    def d_hidden(block):
        rows = slice(block * ROWS, (block + 1) * ROWS)
        part = dot3(pair(dk2, rows, ALL), pair(w2.at[1], ALL, ALL), NT)
        part = part + dot3(pair(dv2, rows, ALL), pair(w2.at[2], ALL, ALL), NT)
        if block == 0:
            part = part + dot3(pair(dq2, ALL, ALL), pair(w2.at[0], ALL, ALL), NT)
        grad = part * gain_row
        hat = xhat[rows]
        inner = jnp.mean(grad * hat, axis=1, keepdims=True)
        return rstd[rows] * (grad - jnp.mean(grad, axis=1, keepdims=True) - hat * inner)

    back = [
        remote(dhalo.at[0], halo_in.at[0], dh_send.at[0], dh_recv.at[0], partner),
        remote(dhalo.at[1], halo_in.at[1], dh_send.at[1], dh_recv.at[1], other),
    ]
    def finish(q):
        arrived(7, q)
        lanes = slice(q * LANES, (q + 1) * LANES)
        dg_acc[...] += (
            full[q, :D] * wf[0, :, lanes] + full[q, D : 2 * D] * wf[1, :, lanes] + full[q, 2 * D : 3 * D] * wf[2, :, lanes]
        )

    dhalo[0] = d_hidden(1)
    step(1, 3)
    step(2, 2)
    step(3, 1)
    step(4, 0)
    dhalo[1] = d_hidden(2)
    step(3, 2)
    step(2, 3)
    step(4, 1)
    step(5, 0)
    dtok_buf[...] = d_hidden(0) + cotf[...]
    step(3, 3)
    step(4, 2)
    step(5, 1)
    step(6, 0)
    res_buf[...] = dot3(pair(o2, ALL, ALL), pair(w2.at[3], ALL, ALL)) + xwin[:ROWS]
    dg_acc[...] = jnp.zeros_like(dg_acc)
    step(4, 3)
    step(5, 2)
    step(6, 1)
    step(7, 0)
    step(6, 2)
    step(5, 3)
    back[0].start()
    back[1].start()
    step(7, 1)
    step(6, 3)
    finish(0)
    step(7, 2)
    finish(1)
    step(7, 3)
    for copy in back:
        copy.wait_recv()
    dtok_buf[...] = dtok_buf[...] + (halo_in[0] + halo_in[1])
    finish(2)
    finish(3)
    d_gain[...] = jnp.sum(dg_acc[...].T, axis=0, keepdims=True) / gain_row
    to_far.wait_send()
    to_near.wait_send()
    for copy in back:
        copy.wait_send()
    for q in range(QUARTERS):
        left_here(6, q)
        left_here(7, q)


def layer(nlist, ncount, tokens, gain, wq, wk, wv, wo, cot):
    vmem = pl.BlockSpec(memory_space=pltpu.VMEM)
    smem = pl.BlockSpec(memory_space=pltpu.SMEM)
    hbm = pl.BlockSpec(memory_space=pl.ANY)
    shape = jax.ShapeDtypeStruct
    dma = pltpu.SemaphoreType.DMA
    v = pltpu.VMEM
    wide = HEADS * LANES
    scratch = [
        v((WIN, D), F32),
        v((4, D, D), F32),
        v((ROWS, D), F32),
        v((WIN, D), F32),
        v((WIN, 1), F32),
        v((2, D, WIN), BF16),
        v((4, 2, D, D), BF16),
        v((2, ROWS, D), BF16),
        v((WIN, wide), BF16),
        v((WIN, wide), BF16),
        v((wide, WIN), BF16),
        v((wide, WIN), BF16),
        v((ROWS, 2 * wide), BF16),
        v((ROWS, 2 * wide), BF16),
        v((D, ROWS), F32),
        v((WIN, ROWS), F32),
        v((2, WIN, D), BF16),
        v((2, WIN, D), BF16),
        v((2, ROWS, D), BF16),
        v((2, ROWS, D), BF16),
        v((4, 2048, LANES), F32),
        v((4, 1024, LANES), F32),
        v((4, 2, 3, 128, LANES), F32),
        v((4, 2, 128, LANES), F32),
        v((4, 2, 3, 32, LANES), F32),
        v((4, 64, LANES), F32),
        v((4, 7, 8, LANES), F32),
        v((2, ROWS, D), F32),
        v((2, ROWS, D), F32),
        v((D, LANES), F32),
        dma((6,)),
        dma((2,)),
        dma((2,)),
    ]
    scratch += [dma((8, QUARTERS)), dma((8, QUARTERS))]
    scratch += [dma((2,)), dma((2,))]
    return pl.pallas_call(
        kernel,
        out_shape=(v((QUARTERS, 2048, LANES), F32), v((ROWS, D), F32), v((ROWS, D), F32), v((1, D), F32)),
        in_specs=[smem] * 2 + [hbm, vmem] + [hbm] * 5,
        out_specs=(vmem,) * 4,
        scratch_shapes=scratch,
        compiler_params=pltpu.CompilerParams(
            collective_id=0, has_side_effects=True, vmem_limit_bytes=52 << 20
        ),
        name="patch_layer",
    )(nlist, ncount, tokens, gain, wq, wk, wv, wo, cot)


def write_kernel(full, res, dtok, gain, result, d_tokens, d_gain, d_q, d_k, d_v, d_o, sem):
    pairs = [(res, result), (dtok, d_tokens), (gain, d_gain)]
    for q in range(QUARTERS):
        lanes = pl.ds(q * LANES, LANES)
        for i, ref in enumerate((d_q, d_k, d_v)):
            pairs.append((full.at[q, pl.ds(i * D, D)], ref.at[:, lanes]))
        for i in range(4):
            pairs.append((full.at[q, pl.ds(3 * D + i * LANES, LANES)], d_o.at[lanes, pl.ds(i * LANES, LANES)]))
    copies = [pltpu.make_async_copy(src, dst, sem.at[i]) for i, (src, dst) in enumerate(pairs)]
    for copy in copies:
        copy.start()
    for copy in copies:
        copy.wait()


def written(full, res, dtok, gain):
    shape = jax.ShapeDtypeStruct
    hbm = pl.BlockSpec(memory_space=pl.ANY)
    vmem = pl.BlockSpec(memory_space=pltpu.VMEM)
    rows, row, square = shape((ROWS, D), F32), shape((1, D), F32), shape((D, D), F32)
    held = [pltpu.with_memory_space_constraint(a, pltpu.VMEM) for a in (full, res, dtok, gain)]
    return pl.pallas_call(
        write_kernel,
        out_shape=(rows, rows, row, square, square, square, square),
        in_specs=[vmem] * 4,
        out_specs=(hbm,) * 7,
        scratch_shapes=[pltpu.SemaphoreType.DMA((3 + 7 * QUARTERS,))],
        compiler_params=pltpu.CompilerParams(vmem_limit_bytes=8 << 20),
        name="write_results",
    )(*held)


def body(tokens, gain, wq, wk, wv, wo, nlist, ncount, cot):
    results = layer(nlist, ncount, tokens, gain[None, :], wq, wk, wv, wo, cot)
    result, d_tokens, d_gain, d_q, d_k, d_v, d_o = written(*results)
    return (result, d_tokens, d_gain[0], d_q, d_k, d_v, d_o)


def solution(mesh):
    rows = P(("space", "slab"), None)
    return jax.shard_map(
        body,
        mesh=mesh,
        in_specs=(rows, P(), P(), P(), P(), P(), rows, P(("space", "slab")), rows),
        out_specs=(rows, rows, P(), P(), P(), P(), P()),
        check_vma=False,
    )
```
